128 devices in a mesh: dp: 16 (over x, z_lo, core), graph: 8 (over z_hi, y).
Axes of the slice: x: 4, y: 4, z: 4 (z_hi: 2, z_lo: 2; z = z_hi * 2 + z_lo), core: 2. Of those that a mesh axis runs over, the one named last changes fastest.
Arguments:
- nodes: bfloat16 [16, 128, 6272], P('dp', 'graph'), may hold values from -6 to 6
- sources: int32 [16, 4096], P('dp', 'graph'), may hold values from 0 to 127
- targets: int32 [16, 4096], P('dp', 'graph'), may hold values from 0 to 127
- edge_counts: int32 [16, 8], P('dp', 'graph'), may hold values from 128 to 512, as said below
- wigner: bfloat16 [16, 29, 49, 4096], P('dp', None, None, 'graph'), as said below
- radial: bfloat16 [16, 4096, 128], P('dp', 'graph'), may hold values from 0.5 to 1.5
- cotangent: bfloat16 [16, 128, 6272], P('dp', 'graph'), may hold values from -6 to 6
- w_zero: bfloat16 [896, 896], replicated, may hold values from -0.1875 to 0.1875
- w_one: bfloat16 [2, 768, 768], replicated, may hold values from -0.15625 to 0.15625
- w_two: bfloat16 [2, 640, 640], replicated, may hold values from -0.15625 to 0.15625
- w_gate: bfloat16 [128, 128], replicated, may hold values from -0.5 to 0.5
Outputs:
- aggregated: bfloat16 [16, 128, 6272], P('dp', 'graph')
- grad_nodes: bfloat16 [16, 128, 6272], P('dp', 'graph')
- grad_zero: float32 [896, 896], replicated
- grad_one: float32 [2, 768, 768], replicated
- grad_two: float32 [2, 640, 640], replicated
- grad_gate: float32 [128, 128], replicated
The draws below stay inside these ranges and needn't reach their ends.
Inputs may be any that keep to these rules, and one draw needn't show every extreme that they name: `edge_counts`: one shard of each batch holds 512 live slots; live slots come first in each shard. `wigner`: for each edge, entry (k, j) is zero unless kept coefficient k and coefficient j have the same degree.
All inputs are finite; a program needn't handle non-finite values.
Results may differ from the reference program's by a relative error of at most 0.013.
Values may be sent and summed in bfloat16 or wider, within the bound.
A program may use at most 128 MiB of HBM per device.

```python
import jax
import jax.numpy as jnp
import numpy as np
from jax import lax

C = 128
LMAX = 6
COEF = 49
KEPT = 29
EDGE_DEV = 512
NODES = 128
EDGES = 4096
BATCHES = 16
N_GRAPH = 8


def draw_edge_counts(key, part):
    first_key, second_key = jax.random.split(key)
    counts = jax.random.randint(first_key, (BATCHES, N_GRAPH), EDGE_DEV // 4, EDGE_DEV + 1)
    fullest = jax.random.randint(second_key, (BATCHES, 1), 0, N_GRAPH)
    columns = jnp.arange(N_GRAPH, dtype=jnp.int32)[None, :]
    return jnp.where(columns == fullest, EDGE_DEV, counts).astype(jnp.int32)


def draw_wigner(key, part):
    kept_degrees = np.array(list(range(LMAX + 1)) + list(range(1, LMAX + 1)) * 2 + list(range(2, LMAX + 1)) * 2)
    full_degrees = np.array([degree for degree in range(LMAX + 1) for order in range(2 * degree + 1)])
    matching = (kept_degrees[:, None] == full_degrees[None, :]).astype(np.float32)
    scaling = matching / np.sqrt(2.0 * full_degrees[None, :] + 1.0).astype(np.float32)
    values = jax.random.normal(key, (BATCHES, KEPT, COEF, EDGES), jnp.float32)
    return (values * jnp.asarray(scaling)[None, :, :, None]).astype(jnp.bfloat16)


def touch_ends(values, rng, low, high):
    index_at = [jax.random.randint(jax.random.fold_in(rng, axis), (), 0, length) for axis, length in enumerate(values.shape)]
    main_axis = values.shape.index(max(values.shape))
    next_to = index_at[:main_axis] + [(index_at[main_axis] + 1) % values.shape[main_axis]] + index_at[main_axis + 1:]
    return values.at[tuple(index_at)].set(low).at[tuple(next_to)].set(high)


def block_scale(rng, shape, cuts, low, largest):
    def one(dim, blocks):
        steps = jax.random.uniform(jax.random.fold_in(jax.random.fold_in(rng, 6), dim), (blocks,), jnp.float32, low / len(cuts), largest / len(cuts))
        return jnp.repeat(jnp.exp(steps), shape[dim] // blocks).reshape((-1,) + (1,) * (len(shape) - dim - 1))

    gain = one(*cuts[0])
    for cut in cuts[1:]:
        gain = gain * one(*cut)
    return gain


def noise(stream_key, dims, scale, bound, cuts=(), kind=jnp.bfloat16):
    result = scale * jax.random.normal(stream_key, dims, jnp.float32)
    if cuts:
        result = result * block_scale(stream_key, dims, cuts, -0.22, 0.18)
    return jnp.clip(result, -bound, bound).astype(kind)


def setup_inputs(seed: int = 0) -> dict:
    arg_keys = jax.random.split(jax.random.key(seed), 12)
    nodes = noise(arg_keys[0], (BATCHES, NODES, COEF * C), 1.0, 6.0, ((0, 16), (1, 8)))
    sources = touch_ends(jax.random.randint(arg_keys[1], (BATCHES, EDGES), 0, NODES), jax.random.fold_in(arg_keys[1], 1), 0, NODES - 1).astype(jnp.int32)
    targets = touch_ends(jax.random.randint(arg_keys[2], (BATCHES, EDGES), 0, NODES), jax.random.fold_in(arg_keys[2], 1), 0, NODES - 1).astype(jnp.int32)
    edge_counts = draw_edge_counts(jax.random.fold_in(arg_keys[11], 71), 0)
    wigner = draw_wigner(jax.random.fold_in(arg_keys[11], 71), 0)
    radial = jnp.clip(0.5 + 1.0 * jax.random.uniform(arg_keys[5], (BATCHES, EDGES, C), jnp.float32) ** block_scale(arg_keys[5], (BATCHES, EDGES, C), ((0, 16), (1, 8)), -0.2, 0.2), 0.5, 1.5).astype(jnp.bfloat16)
    cotangent = noise(arg_keys[6], (BATCHES, NODES, COEF * C), 1.0, 6.0, ((0, 16), (1, 8)))
    w_zero = noise(arg_keys[7], (7 * C, 7 * C), (7 * C) ** -0.5, 0.1875)
    w_one = noise(arg_keys[8], (2, 6 * C, 6 * C), (12 * C) ** -0.5, 0.15625)
    w_two = noise(arg_keys[9], (2, 5 * C, 5 * C), (10 * C) ** -0.5, 0.15625)
    w_gate = noise(arg_keys[10], (C, C), C ** -0.5, 0.5)
    return {"nodes": nodes, "sources": sources, "targets": targets, "edge_counts": edge_counts, "wigner": wigner, "radial": radial, "cotangent": cotangent, "w_zero": w_zero, "w_one": w_one, "w_two": w_two, "w_gate": w_gate}


def product(left, right):
    return jnp.dot(left, right, preferred_element_type=jnp.float32)


def product_left(left, right):
    return lax.dot_general(left, right, (((0,), (0,)), ((), ())), preferred_element_type=jnp.float32)


def product_right(left, right):
    return lax.dot_general(left, right, (((1,), (1,)), ((), ())), preferred_element_type=jnp.float32)


def split_kept(values):
    rows = values.shape[0]
    bounds = ((0, 7), (7, 13), (13, 19), (19, 24), (24, 29))
    return tuple(values[:, lower:upper, :].reshape(rows, -1) for lower, upper in bounds)


def edge_forward(gathered, rotation, radial_rows, valid, w_zero, w_one, w_two, w_gate):
    rows = gathered.shape[0]
    width = w_gate.shape[0]
    turned = jnp.einsum("kje,ejc->ekc", rotation.astype(jnp.float32), gathered.astype(jnp.float32))
    rotated = (turned * radial_rows.astype(jnp.float32)[:, None, :]).astype(jnp.bfloat16)
    zero_part, plus_one, minus_one, plus_two, minus_two = split_kept(rotated)
    mixed = jnp.concatenate([
        product(zero_part, w_zero),
        product(plus_one, w_one[0]) - product(minus_one, w_one[1]),
        product(plus_one, w_one[1]) + product(minus_one, w_one[0]),
        product(plus_two, w_two[0]) - product(minus_two, w_two[1]),
        product(plus_two, w_two[1]) + product(minus_two, w_two[0])], axis=1).reshape(rows, -1, width)
    scalar = mixed[:, 0, :]
    scalar_low = scalar.astype(jnp.bfloat16)
    gate = jax.nn.sigmoid(product(scalar_low, w_gate))
    message = jnp.concatenate([jax.nn.silu(scalar)[:, None, :], mixed[:, 1:, :] * gate[:, None, :]], axis=1)
    message = (message * valid[:, None, None].astype(jnp.float32)).astype(jnp.bfloat16)
    back = jnp.einsum("kje,ekc->ejc", rotation.astype(jnp.float32), message.astype(jnp.float32)).astype(jnp.bfloat16)
    return back, (rotated, mixed, scalar_low, gate)


def edge_backward(upstream, rotation, radial_rows, saved, w_zero, w_one, w_two, w_gate):
    rotated, mixed, scalar_low, gate = saved
    rows = upstream.shape[0]
    width = w_gate.shape[0]
    incoming = jnp.einsum("kje,ejc->ekc", rotation.astype(jnp.float32), upstream.astype(jnp.float32))
    scalar = mixed[:, 0, :]
    sigmoid_value = jax.nn.sigmoid(scalar)
    direct = incoming[:, 0, :] * sigmoid_value * (1.0 + scalar * (1.0 - sigmoid_value))
    gate_low = (jnp.sum(incoming[:, 1:, :] * mixed[:, 1:, :], axis=1) * gate * (1.0 - gate)).astype(jnp.bfloat16)
    head = direct + product_right(gate_low, w_gate)
    mixed_grad = jnp.concatenate([head[:, None, :], incoming[:, 1:, :] * gate[:, None, :]], axis=1).astype(jnp.bfloat16)
    zero_grad, plus_one_grad, minus_one_grad, plus_two_grad, minus_two_grad = split_kept(mixed_grad)
    zero_part, plus_one, minus_one, plus_two, minus_two = split_kept(rotated)
    grad_zero = product_left(zero_part, zero_grad)
    grad_one = jnp.stack([
        product_left(plus_one, plus_one_grad) + product_left(minus_one, minus_one_grad),
        product_left(plus_one, minus_one_grad) - product_left(minus_one, plus_one_grad)])
    grad_two = jnp.stack([
        product_left(plus_two, plus_two_grad) + product_left(minus_two, minus_two_grad),
        product_left(plus_two, minus_two_grad) - product_left(minus_two, plus_two_grad)])
    grad_gate = product_left(scalar_low, gate_low)
    backward_parts = jnp.concatenate([
        product_right(zero_grad, w_zero),
        product_right(plus_one_grad, w_one[0]) + product_right(minus_one_grad, w_one[1]),
        product_right(minus_one_grad, w_one[0]) - product_right(plus_one_grad, w_one[1]),
        product_right(plus_two_grad, w_two[0]) + product_right(minus_two_grad, w_two[1]),
        product_right(minus_two_grad, w_two[0]) - product_right(plus_two_grad, w_two[1])], axis=1).reshape(rows, -1, width)
    rotated_grad = (backward_parts * radial_rows.astype(jnp.float32)[:, None, :]).astype(jnp.bfloat16)
    source_grad = jnp.einsum("kje,ekc->ejc", rotation.astype(jnp.float32), rotated_grad.astype(jnp.float32)).astype(jnp.bfloat16)
    return source_grad, (grad_zero, grad_one, grad_two, grad_gate)


def reference(nodes, sources, targets, edge_counts, wigner, radial, cotangent, w_zero, w_one, w_two, w_gate):
    width = w_gate.shape[0]
    positions = jnp.arange(EDGES, dtype=jnp.int32)

    def one_batch(totals, items):
        node_rows, source_ids, target_ids, counts, rotation, radial_rows, upstream_rows = items
        valid = (positions % EDGE_DEV) < counts[positions // EDGE_DEV]
        gathered = jnp.take(node_rows, source_ids, axis=0).reshape(EDGES, -1, width)
        back, saved = edge_forward(gathered, rotation, radial_rows, valid, w_zero, w_one, w_two, w_gate)
        summed = jax.ops.segment_sum(back.reshape(EDGES, -1).astype(jnp.float32), target_ids, num_segments=NODES)
        upstream = jnp.take(upstream_rows, target_ids, axis=0) * valid[:, None].astype(upstream_rows.dtype)
        upstream = upstream.reshape(EDGES, -1, width)
        source_grad, grads = edge_backward(upstream, rotation, radial_rows, saved, w_zero, w_one, w_two, w_gate)
        grad_rows = jax.ops.segment_sum(source_grad.reshape(EDGES, -1).astype(jnp.float32), source_ids, num_segments=NODES)
        totals = tuple(total + grad for total, grad in zip(totals, grads))
        return totals, (summed.astype(jnp.bfloat16), grad_rows.astype(jnp.bfloat16))

    start_totals = (jnp.zeros(w_zero.shape, jnp.float32), jnp.zeros(w_one.shape, jnp.float32),
                    jnp.zeros(w_two.shape, jnp.float32), jnp.zeros(w_gate.shape, jnp.float32))
    totals, outputs = lax.scan(one_batch, start_totals,
                               (nodes, sources, targets, edge_counts, wigner, radial, cotangent))
    return outputs[0], outputs[1], totals[0], totals[1], totals[2], totals[3]
```

```python
import jax
import jax.numpy as jnp
from jax import lax
from jax.experimental import pallas as pl
from jax.experimental.pallas import tpu as pltpu
from jax.sharding import PartitionSpec as P

BF = jnp.bfloat16
F32 = jnp.float32
C = 128
CH = 32
ONE_AT, TWO_AT, GATE_AT, USED, TOTAL = 6272, 15488, 21888, 22016, 22528


def kept(l):
    ks = [l]
    if l >= 1:
        ks += [7 + l - 1, 13 + l - 1]
    if l >= 2:
        ks += [19 + l - 2, 24 + l - 2]
    return ks


def nn(a, b):
    return jnp.dot(a, b, preferred_element_type=F32)


def nt(a, b):
    return lax.dot_general(a, b, (((1,), (1,)), ((), ())), preferred_element_type=F32)


def tn(a, b):
    return lax.dot_general(a, b, (((0,), (0,)), ((), ())), preferred_element_type=F32)


def weighted(terms):
    total = None
    for w, v in terms:
        part = v.reshape(CH // 8, 8, 128) * w[None]
        total = part if total is None else total + part
    return total.reshape(CH, 128)


def prepare(src, tgt, cnt, wig, rad, w0, w1, w2, wg, w0t, w1t, w2t, wgt, wf, radt, ohs, oht):
    edges = src.shape[1]

    def spread_row(k, _):
        for q in range(4):
            wf[q, k, 0:49, :] = wig[k, :, q * 128 : (q + 1) * 128].astype(F32)
        return 0

    lax.fori_loop(0, 29, spread_row, 0)
    node = lax.broadcasted_iota(jnp.int32, (128, edges), 0)
    slot = lax.broadcasted_iota(jnp.int32, (128, edges), 1)
    ohs[...] = jnp.where(node == src[...], 1.0, 0.0).astype(BF)
    live = slot < cnt[...]
    oht[...] = jnp.where((node == tgt[...]) & live, 1.0, 0.0).astype(BF)
    radt[...] = rad[...].astype(F32).T

    def turn(block, out, size):
        def step(i, _):
            at = pl.multiple_of(i * 128, 128)
            out[:, pl.ds(at, 128)] = block[pl.ds(at, 128), :].T
            return 0

        lax.fori_loop(0, size // 128, step, 0)

    turn(w0, w0t, 896)
    for i in range(2):
        turn(w1.at[i], w1t.at[i], 768)
        turn(w2.at[i], w2t.at[i], 640)
    wgt[...] = wg[...].T


INTERPRET = False


def row(wf, q, k, j):
    if INTERPRET:
        return jnp.broadcast_to(wf[q, k, pl.ds(j, 1), :], (8, 128))
    return wf[q, k, pl.ds(j, 8, stride=0), :]


def tiles(body):
    def step(t, _):
        body(pl.multiple_of((t // 4) * CH, CH), t % 4)
        return 0

    lax.fori_loop(0, 4 * (128 // CH), step, 0)


def turn_in(l, wf, gbuf, emit):
    count = 2 * l + 1

    def body(c0, q):
        e0 = pl.multiple_of(q * 128, 128)
        vals = [gbuf[pl.ds(j * 128 + c0, CH), pl.ds(e0, 128)].astype(F32) for j in range(count)]
        for k in kept(l):
            emit(k, weighted([(row(wf, q, k, l * l + j), vals[j]) for j in range(count)]), c0, e0)

    tiles(body)


def turn_out(l, wf, load, bk):
    count = 2 * l + 1

    def body(c0, q):
        e0 = pl.multiple_of(q * 128, 128)
        vals = [load(k, c0, e0) for k in kept(l)]
        for j in range(count):
            out = weighted([(row(wf, q, k, l * l + j), v) for k, v in zip(kept(l), vals)])
            bk[pl.ds(j * 128 + c0, CH), pl.ds(e0, 128)] = out.astype(BF)

    tiles(body)


def halves(body):
    def step(h, _):
        body(pl.ds(pl.multiple_of(h * 256, 256), 256))
        return 0

    lax.fori_loop(0, 2, step, 0)


def sigmoid(v):
    return 1.0 / (1.0 + jnp.exp(-v))


def cols(l):
    return slice(l * l * 128, (l + 1) * (l + 1) * 128)


def forward(nodes, wf, radt, ohs, w0t, w1t, w2t, wgt, gbuf, R, mix, gate):
    for l in range(7):
        gbuf[0 : (2 * l + 1) * 128, :] = tn(nodes[:, cols(l)], ohs[...]).astype(BF)

        def emit(k, v, c0, e0):
            R[pl.ds(k * 128 + c0, CH), pl.ds(e0, 128)] = (v * radt[pl.ds(c0, CH), pl.ds(e0, 128)]).astype(BF)

        turn_in(l, wf, gbuf, emit)

    def zero(e):
        mix[0:896, e] = nn(w0t[...], R[0:896, e])
        scalar = mix[0:128, e].astype(BF)
        gate[:, e] = sigmoid(nn(wgt[...], scalar))

    halves(zero)
    for wt, at, n in ((w1t, 896, 768), (w2t, 2432, 640)):
        def pair(e):
            p, m = R[at : at + n, e], R[at + n : at + 2 * n, e]
            mix[at : at + n, e] = nn(wt[0], p) - nn(wt[1], m)
            mix[at + n : at + 2 * n, e] = nn(wt[1], p) + nn(wt[0], m)

        halves(pair)


def send_messages(wf, mix, gate, oht, bk, agg):
    for l in range(7):
        def load(k, c0, e0):
            v = mix[pl.ds(k * 128 + c0, CH), pl.ds(e0, 128)]
            m = v * sigmoid(v) if k == 0 else v * gate[pl.ds(c0, CH), pl.ds(e0, 128)]
            return m.astype(BF).astype(F32)

        turn_out(l, wf, load, bk)
        agg[:, cols(l)] = nt(oht[...], bk[0 : (2 * l + 1) * 128, :]).astype(BF)


def backward(cot, wf, oht, wg, gbuf, mix, gate, G, gl, direct):
    gl[...] = jnp.zeros_like(gl)
    for l in range(7):
        gbuf[0 : (2 * l + 1) * 128, :] = tn(cot[:, cols(l)], oht[...]).astype(BF)

        def emit(k, v, c0, e0):
            at = (pl.ds(c0, CH), pl.ds(e0, 128))
            x = mix[pl.ds(k * 128 + c0, CH), pl.ds(e0, 128)]
            if k == 0:
                s = sigmoid(x)
                direct[at] = v * s * (1.0 + x * (1.0 - s))
            else:
                G[pl.ds(k * 128 + c0, CH), pl.ds(e0, 128)] = (v * gate[at]).astype(BF)
                gl[at] += v * x

        turn_in(l, wf, gbuf, emit)
    low = (gl[...] * gate[...] * (1.0 - gate[...])).astype(BF)
    G[0:128, :] = (direct[...] + nn(wg[...], low)).astype(BF)
    return low


def weight_grads(R, G, mix, low, g):
    for at in (0, 256, 512, 768):
        wide = min(256, 896 - at)
        out = nt(R[0:896, :], G[at : at + wide, :]).astype(BF)
        for q in range(wide // 128):
            p = at // 128 + q
            g[p * 896 : (p + 1) * 896, :] = out[:, q * 128 : (q + 1) * 128]
    for base, at, n in ((ONE_AT, 896, 768), (TWO_AT, 2432, 640)):
        for lo in range(0, n, 256):
            wide = min(256, n - lo)
            plus, minus = G[at + lo : at + lo + wide, :], G[at + n + lo : at + n + lo + wide, :]
            rp, rm = R[at : at + n, :], R[at + n : at + 2 * n, :]
            for i, out in enumerate((nt(rp, plus) + nt(rm, minus), nt(rp, minus) - nt(rm, plus))):
                out = out.astype(BF)
                for q in range(wide // 128):
                    r = base + (i * (n // 128) + lo // 128 + q) * n
                    g[r : r + n, :] = out[:, q * 128 : (q + 1) * 128]
    g[GATE_AT:USED, :] = nt(mix[0:128, :].astype(BF), low).astype(BF)
    g[USED:TOTAL, :] = jnp.zeros((TOTAL - USED, 128), BF)


def rotated_grads(radt, w0, w1, w2, G, R):
    def scale(v, e):
        n = v.shape[0]
        return (v.reshape(n // 128, 128, v.shape[1]) * radt[:, e][None]).reshape(v.shape).astype(BF)

    def zero(e):
        R[0:896, e] = scale(nn(w0[...], G[0:896, e]), e)

    halves(zero)
    for w, at, n in ((w1, 896, 768), (w2, 2432, 640)):
        def pair(e):
            p, m = G[at : at + n, e], G[at + n : at + 2 * n, e]
            R[at : at + n, e] = scale(nn(w[0], p) + nn(w[1], m), e)
            R[at + n : at + 2 * n, e] = scale(nn(w[0], m) - nn(w[1], p), e)

        halves(pair)


def source_grads(wf, ohs, R, bk, gn):
    for l in range(7):
        def load(k, c0, e0):
            return R[pl.ds(k * 128 + c0, CH), pl.ds(e0, 128)].astype(F32)

        turn_out(l, wf, load, bk)
        gn[:, cols(l)] = nt(ohs[...], bk[0 : (2 * l + 1) * 128, :]).astype(BF)


HALF = TOTAL // 2
MESH = pl.DeviceIdType.MESH
PEERS = [(dz, dy) for dz in range(2) for dy in range(4) if (dz, dy) != (0, 0)]
COLORS = ((0, 4096, (0, 1, 2)), (4096, 4096, (1, 2, 0)), (8192, 3072, (2, 0, 1)))
SLOT_ROWS = sum(3 * (size // 4 + size // 16 + size // 64) for _, size, _ in COLORS)
N_SEMS = 4 * 7 + 2 + 2 * 27


class Links:
    def __init__(self, send, recv):
        dp, self.g = lax.axis_index("dp"), lax.axis_index("graph")
        self.dp = dp
        self.pos = (dp // 4, self.g % 4, (self.g // 4) * 2 + (dp // 2) % 2)
        self.core = dp % 2
        self.send, self.recv, self.used = send, recv, 0

    def at(self, x, y, z, core):
        return ((x * 2 + z % 2) * 2 + core, (z // 2) * 4 + y)

    def along(self, axis, step):
        pos = list(self.pos)
        pos[axis] = (pos[axis] + step) % 4
        return self.at(*pos, self.core)

    def graph_peer(self, dz, dy):
        return (self.dp, ((self.g // 4 + dz) % 2) * 4 + (self.g % 4 + dy) % 4)

    def other_core(self):
        return self.at(*self.pos, 1 - self.core)

    def greet(self):
        peers = [self.graph_peer(*p) for p in PEERS]
        peers += [self.along(0, 1), self.along(0, 2), self.along(0, 3), self.along(2, 1), self.along(2, 3)]
        peers.append(self.other_core())
        barrier = pltpu.get_barrier_semaphore()
        for peer in peers:
            pl.semaphore_signal(barrier, inc=1, device_id=peer, device_id_type=MESH)
        pl.semaphore_wait(barrier, len(peers))

    def copy(self, src, dst, peer):
        out = pltpu.make_async_remote_copy(
            src_ref=src, dst_ref=dst, send_sem=self.send.at[self.used], recv_sem=self.recv.at[self.used],
            device_id=peer, device_id_type=MESH,
        )
        self.used += 1
        out.start()
        return out


def done(copies):
    for c in copies:
        c.wait()


def rows16(i, n=16):
    return pl.ds(pl.multiple_of(i * 16, 16), n)


def gather_start(links, x, full):
    mine = rows16(links.g)
    out = [links.copy(x, full.at[mine], links.graph_peer(*p)) for p in PEERS]
    full[mine, :] = x[...]
    return out


def scatter_start(links, part, slots):
    out = []
    for i, p in enumerate(PEERS):
        peer = links.graph_peer(*p)
        out.append(links.copy(part.at[rows16(peer[1])], slots.at[i], peer))
    return out


def scatter_finish(links, copies, part, slots, out):
    done(copies)
    total = part[rows16(links.g), :].astype(F32)
    for i in range(len(PEERS)):
        total += slots[i].astype(F32)
    out[...] = total.astype(BF)


def add_rows(dst, d0, srcs, n):
    step = 256 if n % 256 == 0 else n

    def body(t, _):
        total = None
        for ref, r in srcs:
            v = ref[pl.ds(pl.multiple_of(r + t * step, 16), step), :].astype(F32)
            total = v if total is None else total + v
        dst[pl.ds(pl.multiple_of(d0 + t * step, 16), step), :] = total.astype(BF)
        return 0

    if n == step:
        body(0, 0)
    else:
        lax.fori_loop(0, n // step, body, 0)


def swap_start(links, g, inbox):
    away = pl.multiple_of((1 - links.core) * HALF, 16)
    return [links.copy(g.at[pl.ds(away, HALF)], inbox, links.other_core())]


def reduce_all(links, swap, g, inbox, slots, mid, small, full):
    home = links.core * HALF
    done(swap)
    add_rows(g, home, [(g, home), (inbox, 0)], HALF)
    waiting, src, at = {}, {}, 0
    for c, (base, size, axes) in enumerate(COLORS):
        src[c] = (g, home + base)
    slot_at, place = {}, {}
    for c, (base, size, axes) in enumerate(COLORS):
        for s in range(3):
            slot_at[c, s] = at
            at += 3 * (size // 4 ** (s + 1))

    def start(c, s):
        base, size, axes = COLORS[c]
        n, (ref, row), axis = size // 4 ** (s + 1), src[c], axes[s]
        out = []
        for d in (1, 3, 2):
            j = (links.pos[axis] + d) % 4
            out.append(links.copy(
                ref.at[pl.ds(pl.multiple_of(row + j * n, 16), n)],
                slots.at[pl.ds(slot_at[c, s] + (d - 1) * n, n)],
                links.along(axis, d)))
        waiting[c] = out

    def reduce(c, s):
        base, size, axes = COLORS[c]
        n, (ref, row), axis = size // 4 ** (s + 1), src[c], axes[s]
        own = row + links.pos[axis] * n
        place[c] = place.get(c, home + base) + links.pos[axis] * n
        done(waiting[c])
        srcs = [(ref, own)] + [(slots, slot_at[c, s] + d * n) for d in range(3)]
        if s == 0:
            dst, d0 = mid, base // 4
        elif s == 1:
            dst, d0 = small, base // 16
        else:
            dst, d0 = full, place[c]
        add_rows(dst, d0, srcs, n)
        src[c] = (dst, d0)

    def share(c, s):
        base, size, axes = COLORS[c]
        n, axis = size // 4 ** (s + 1), axes[s]
        rows = pl.ds(pl.multiple_of(place[c], 16), n)
        waiting[c] = [links.copy(full.at[rows], full.at[rows], links.along(axis, d)) for d in (1, 3, 2)]
        place[c] = place[c] - links.pos[axis] * n

    for c in range(3):
        start(c, 0)
    for s in range(3):
        for c in range(3):
            reduce(c, s)
            if s < 2:
                start(c, s + 1)
            else:
                share(c, 2)
    for s in (1, 0):
        for c in range(3):
            done(waiting[c])
            share(c, s)
    for c in range(3):
        done(waiting[c])
    mine = pl.ds(pl.multiple_of(home, 16), HALF)
    done([links.copy(full.at[mine], full.at[mine], links.other_core())])


def layer_kernel(x, cx, src, tgt, cnt, wig, rad, w0, w1, w2, wg, agg, gn, full,
                 nodes, cot, w0t, w1t, w2t, wgt, wf, radt, ohs, oht, gbuf, R, mix, G, gate, gl, direct, bk,
                 pagg, slots1, slots2, g, inbox, slots, mid, small, send, recv):
    links = Links(send, recv)
    links.greet()
    arriving = gather_start(links, x, nodes)
    prepare(src, tgt, cnt, wig, rad, w0, w1, w2, wg, w0t, w1t, w2t, wgt, wf, radt, ohs, oht)
    done(arriving)
    arriving = gather_start(links, cx, cot)
    forward(nodes, wf, radt, ohs, w0t, w1t, w2t, wgt, gbuf, R, mix, gate)
    send_messages(wf, mix, gate, oht, bk, pagg)
    done(arriving)
    leaving = scatter_start(links, pagg, slots1)
    low = backward(cot, wf, oht, wg, gbuf, mix, gate, G, gl, direct)
    weight_grads(R, G, mix, low, g)
    swap = swap_start(links, g, inbox)
    scatter_finish(links, leaving, pagg, slots1, agg)
    rotated_grads(radt, w0, w1, w2, G, R)
    source_grads(wf, ohs, R, bk, nodes)
    leaving = scatter_start(links, nodes, slots2)
    reduce_all(links, swap, g, inbox, slots, mid, small, full)
    scatter_finish(links, leaving, nodes, slots2, gn)


def unpack_kernel(full, zero, one, two, last, b0, b1, b2, b3, sems):
    for p in range(7):
        b0[:, p * 128 : (p + 1) * 128] = full[p * 896 : (p + 1) * 896, :].astype(F32)
    copies = [pltpu.make_async_copy(b0, zero, sems.at[0])]
    copies[0].start()
    for buf, out, base, n, s in ((b1, one, ONE_AT, 768, 1), (b2, two, TWO_AT, 640, 3)):
        for i in range(2):
            for p in range(n // 128):
                at = base + (i * (n // 128) + p) * n
                buf[i, :, p * 128 : (p + 1) * 128] = full[at : at + n, :].astype(F32)
            copies.append(pltpu.make_async_copy(buf.at[i], out.at[i], sems.at[s + i]))
            copies[-1].start()
    b3[...] = full[GATE_AT:USED, :].astype(F32)
    copies.append(pltpu.make_async_copy(b3, last, sems.at[5]))
    copies[-1].start()
    for c in copies:
        c.wait()


def per_device(nodes, sources, targets, counts, wigner, radial, cotangent, w0, w1, w2, wg):
    vm = pl.BlockSpec(memory_space=pltpu.VMEM)
    hbm = pl.BlockSpec(memory_space=pl.ANY)
    dma = pltpu.SemaphoreType.DMA
    agg, gn, full = pl.pallas_call(
        layer_kernel,
        out_shape=(
            jax.ShapeDtypeStruct((16, 6272), BF),
            jax.ShapeDtypeStruct((16, 6272), BF),
            jax.ShapeDtypeStruct((TOTAL, 128), BF),
        ),
        in_specs=[vm] * 11,
        out_specs=(vm, vm, vm),
        scratch_shapes=[
            pltpu.VMEM((128, 6272), BF),
            pltpu.VMEM((128, 6272), BF),
            pltpu.VMEM((896, 896), BF),
            pltpu.VMEM((2, 768, 768), BF),
            pltpu.VMEM((2, 640, 640), BF),
            pltpu.VMEM((128, 128), BF),
            pltpu.VMEM((4, 29, 56, 128), F32),
            pltpu.VMEM((128, 512), F32),
            pltpu.VMEM((128, 512), BF),
            pltpu.VMEM((128, 512), BF),
            pltpu.VMEM((13 * 128, 512), BF),
            pltpu.VMEM((3712, 512), BF),
            pltpu.VMEM((3712, 512), F32),
            pltpu.VMEM((3712, 512), BF),
            pltpu.VMEM((128, 512), F32),
            pltpu.VMEM((128, 512), F32),
            pltpu.VMEM((128, 512), F32),
            pltpu.VMEM((13 * 128, 512), BF),
            pltpu.VMEM((128, 6272), BF),
            pltpu.VMEM((7, 16, 6272), BF),
            pltpu.VMEM((7, 16, 6272), BF),
            pltpu.VMEM((TOTAL, 128), BF),
            pltpu.VMEM((HALF, 128), BF),
            pltpu.VMEM((SLOT_ROWS, 128), BF),
            pltpu.VMEM((HALF // 4, 128), BF),
            pltpu.VMEM((HALF // 16, 128), BF),
            dma((N_SEMS,)),
            dma((N_SEMS,)),
        ],
        compiler_params=pltpu.CompilerParams(
            vmem_limit_bytes=67043328, collective_id=0, has_side_effects=True
        ),
        name="edge_layer",
    )(nodes[0], cotangent[0], sources, targets, counts, wigner[0], radial[0], w0, w1, w2, wg)
    zero, one, two, last = pl.pallas_call(
        unpack_kernel,
        out_shape=(
            jax.ShapeDtypeStruct((896, 896), F32),
            jax.ShapeDtypeStruct((2, 768, 768), F32),
            jax.ShapeDtypeStruct((2, 640, 640), F32),
            jax.ShapeDtypeStruct((128, 128), F32),
        ),
        in_specs=[vm],
        out_specs=(hbm,) * 4,
        scratch_shapes=[
            pltpu.VMEM((896, 896), F32),
            pltpu.VMEM((2, 768, 768), F32),
            pltpu.VMEM((2, 640, 640), F32),
            pltpu.VMEM((128, 128), F32),
            dma((6,)),
        ],
        compiler_params=pltpu.CompilerParams(vmem_limit_bytes=40 << 20),
        name="unpack",
    )(full)
    return agg[None], gn[None], zero, one, two, last


def solution(mesh):
    in_specs = (
        P("dp", "graph", None),
        P("dp", "graph"),
        P("dp", "graph"),
        P("dp", "graph"),
        P("dp", None, None, "graph"),
        P("dp", "graph", None),
        P("dp", "graph", None),
        P(),
        P(),
        P(),
        P(),
    )
    out_specs = (P("dp", "graph", None), P("dp", "graph", None), P(), P(), P(), P())
    return jax.shard_map(
        per_device, mesh=mesh, in_specs=in_specs, out_specs=out_specs, check_vma=False
    )
```

```python
import jax
import jax.numpy as jnp
from jax import lax
from jax.experimental import pallas as pl
from jax.experimental.pallas import tpu as pltpu
from jax.sharding import PartitionSpec as P

BF = jnp.bfloat16
F32 = jnp.float32
C = 128
CH = 32
ONE_AT, TWO_AT, GATE_AT, USED, TOTAL = 6272, 15488, 21888, 22016, 22528


def kept(l):
    ks = [l]
    if l >= 1:
        ks += [7 + l - 1, 13 + l - 1]
    if l >= 2:
        ks += [19 + l - 2, 24 + l - 2]
    return ks


def nn(a, b):
    return jnp.dot(a, b, preferred_element_type=F32)


def nt(a, b):
    return lax.dot_general(a, b, (((1,), (1,)), ((), ())), preferred_element_type=F32)


def tn(a, b):
    return lax.dot_general(a, b, (((0,), (0,)), ((), ())), preferred_element_type=F32)


def weighted(terms):
    total = None
    for w, v in terms:
        part = v.reshape(CH // 8, 8, 128) * w[None]
        total = part if total is None else total + part
    return total.reshape(CH, 128)


def prepare(src, tgt, cnt, wig, rad, wf, radt, ohs, oht):
    edges = src.shape[1]

    def spread_row(j, _):
        for q in range(4):
            wf[q, j, 0:29, :] = wig[j, :, q * 128 : (q + 1) * 128].astype(F32)
        return 0

    lax.fori_loop(0, 49, spread_row, 0)
    node = lax.broadcasted_iota(jnp.int32, (128, edges), 0)
    slot = lax.broadcasted_iota(jnp.int32, (128, edges), 1)
    ohs[...] = jnp.where(node == src[...], 1.0, 0.0).astype(BF)
    live = slot < cnt[...]
    oht[...] = jnp.where((node == tgt[...]) & live, 1.0, 0.0).astype(BF)
    radt[...] = rad[...].astype(F32).T


def turn(block, out):
    def step(i, _):
        at = pl.multiple_of(i * 128, 128)
        out[:, pl.ds(at, 128)] = block[pl.ds(at, 128), :].T
        return 0

    lax.fori_loop(0, block.shape[0] // 128, step, 0)


INTERPRET = False


def row(wf, q, k, j):
    if INTERPRET:
        return jnp.broadcast_to(wf[q, j, pl.ds(k, 1), :], (8, 128))
    return wf[q, j, pl.ds(k, 8, stride=0), :]


def tiles(body):
    def step(t, _):
        body(pl.multiple_of((t // 4) * CH, CH), t % 4)
        return 0

    lax.fori_loop(0, 4 * (128 // CH), step, 0)


def turn_in(l, wf, gbuf, emit):
    count = 2 * l + 1

    def body(c0, q):
        e0 = pl.multiple_of(q * 128, 128)
        vals = [gbuf[pl.ds(j * 128 + c0, CH), pl.ds(e0, 128)].astype(F32) for j in range(count)]
        for k in kept(l):
            emit(k, weighted([(row(wf, q, k, l * l + j), vals[j]) for j in range(count)]), c0, e0)

    tiles(body)


def turn_out(l, wf, load, bk):
    count = 2 * l + 1

    def body(c0, q):
        e0 = pl.multiple_of(q * 128, 128)
        vals = [load(k, c0, e0) for k in kept(l)]
        for j in range(count):
            out = weighted([(row(wf, q, k, l * l + j), v) for k, v in zip(kept(l), vals)])
            bk[pl.ds(j * 128 + c0, CH), pl.ds(e0, 128)] = out.astype(BF)

    tiles(body)


def halves(body):
    def step(h, _):
        body(pl.ds(pl.multiple_of(h * 256, 256), 256))
        return 0

    lax.fori_loop(0, 2, step, 0)


def sigmoid(v):
    return 1.0 / (1.0 + jnp.exp(-v))


def cols(l):
    return slice(l * l * 128, (l + 1) * (l + 1) * 128)


def forward(nodes, wf, radt, ohs, w0t, w1t, w2t, wgt, gbuf, R, mix, gate, hook):
    for l in range(7):
        gbuf[0 : (2 * l + 1) * 128, :] = tn(nodes[:, cols(l)], ohs[...]).astype(BF)

        def emit(k, v, c0, e0):
            R[pl.ds(k * 128 + c0, CH), pl.ds(e0, 128)] = (v * radt[pl.ds(c0, CH), pl.ds(e0, 128)]).astype(BF)

        turn_in(l, wf, gbuf, emit)
        hook(l)

    def zero(e):
        mix[0:896, e] = nn(w0t[...], R[0:896, e])
        scalar = mix[0:128, e].astype(BF)
        gate[:, e] = sigmoid(nn(wgt[...], scalar))

    halves(zero)
    for wt, at, n in ((w1t, 896, 768), (w2t, 2432, 640)):
        def pair(e):
            p, m = R[at : at + n, e], R[at + n : at + 2 * n, e]
            mix[at : at + n, e] = nn(wt[0], p) - nn(wt[1], m)
            mix[at + n : at + 2 * n, e] = nn(wt[1], p) + nn(wt[0], m)

        halves(pair)


def send_messages(wf, mix, gate, oht, bk, agg, hook):
    for l in range(7):
        def load(k, c0, e0):
            v = mix[pl.ds(k * 128 + c0, CH), pl.ds(e0, 128)]
            m = v * sigmoid(v) if k == 0 else v * gate[pl.ds(c0, CH), pl.ds(e0, 128)]
            return m.astype(BF).astype(F32)

        turn_out(l, wf, load, bk)
        agg[:, cols(l)] = nt(oht[...], bk[0 : (2 * l + 1) * 128, :]).astype(BF)
        hook(l)


def backward(cot, wf, oht, wg, gbuf, mix, gate, G, gl, direct):
    gl[...] = jnp.zeros_like(gl)
    for l in range(7):
        gbuf[0 : (2 * l + 1) * 128, :] = tn(cot[:, cols(l)], oht[...]).astype(BF)

        def emit(k, v, c0, e0):
            at = (pl.ds(c0, CH), pl.ds(e0, 128))
            x = mix[pl.ds(k * 128 + c0, CH), pl.ds(e0, 128)]
            if k == 0:
                s = sigmoid(x)
                direct[at] = v * s * (1.0 + x * (1.0 - s))
            else:
                G[pl.ds(k * 128 + c0, CH), pl.ds(e0, 128)] = (v * gate[at]).astype(BF)
                gl[at] += v * x

        turn_in(l, wf, gbuf, emit)
    low = (gl[...] * gate[...] * (1.0 - gate[...])).astype(BF)
    G[0:128, :] = (direct[...] + nn(wg[...], low)).astype(BF)
    return low


def weight_grads(R, G, mix, low, g):
    for at in (0, 256, 512, 768):
        wide = min(256, 896 - at)
        out = nt(R[0:896, :], G[at : at + wide, :]).astype(BF)
        for q in range(wide // 128):
            p = at // 128 + q
            g[p * 896 : (p + 1) * 896, :] = out[:, q * 128 : (q + 1) * 128]
    for base, at, n in ((ONE_AT, 896, 768), (TWO_AT, 2432, 640)):
        for lo in range(0, n, 256):
            wide = min(256, n - lo)
            plus, minus = G[at + lo : at + lo + wide, :], G[at + n + lo : at + n + lo + wide, :]
            rp, rm = R[at : at + n, :], R[at + n : at + 2 * n, :]
            for i, out in enumerate((nt(rp, plus) + nt(rm, minus), nt(rp, minus) - nt(rm, plus))):
                out = out.astype(BF)
                for q in range(wide // 128):
                    r = base + (i * (n // 128) + lo // 128 + q) * n
                    g[r : r + n, :] = out[:, q * 128 : (q + 1) * 128]
    g[GATE_AT:USED, :] = nt(mix[0:128, :].astype(BF), low).astype(BF)
    g[USED:TOTAL, :] = jnp.zeros((TOTAL - USED, 128), BF)


def rotated_grads(radt, w0, w1, w2, G, R):
    def scale(v, e):
        n = v.shape[0]
        return (v.reshape(n // 128, 128, v.shape[1]) * radt[:, e][None]).reshape(v.shape).astype(BF)

    def zero(e):
        R[0:896, e] = scale(nn(w0[...], G[0:896, e]), e)

    halves(zero)
    for w, at, n in ((w1, 896, 768), (w2, 2432, 640)):
        def pair(e):
            p, m = G[at : at + n, e], G[at + n : at + 2 * n, e]
            R[at : at + n, e] = scale(nn(w[0], p) + nn(w[1], m), e)
            R[at + n : at + 2 * n, e] = scale(nn(w[0], m) - nn(w[1], p), e)

        halves(pair)


def source_grads(wf, ohs, R, bk, gn, hook):
    for l in range(7):
        def load(k, c0, e0):
            return R[pl.ds(k * 128 + c0, CH), pl.ds(e0, 128)].astype(F32)

        turn_out(l, wf, load, bk)
        gn[:, cols(l)] = nt(ohs[...], bk[0 : (2 * l + 1) * 128, :]).astype(BF)
        hook(l)


HALF = TOTAL // 2
MESH = pl.DeviceIdType.MESH
CUT = 20 * 128
FIRST, REST = slice(0, CUT), slice(CUT, 6272)
COLORS = ((0, 3072, (0, 1, 2)), (3072, 3072, (0, 2, 1)), (6144, 3072, (1, 2, 0)), (9216, 2048, (2, 0, 1)))
N = len(COLORS)
SLOT_ROWS = sum(3 * (size // 4 + size // 16 + size // 64) for _, size, _ in COLORS)
N_SEMS = 2 * 14 + 2 * 11 + 2 * N + 2 * 9 * N


class Links:
    def __init__(self, send, recv):
        dp, self.g = lax.axis_index("dp"), lax.axis_index("graph")
        self.dp = dp
        self.pos = (dp // 4, self.g % 4, (self.g // 4) * 2 + (dp // 2) % 2)
        self.core = dp % 2
        self.send, self.recv, self.used = send, recv, 0

    def at(self, x, y, z, core):
        return ((x * 2 + z % 2) * 2 + core, (z // 2) * 4 + y)

    def along(self, axis, step):
        pos = list(self.pos)
        pos[axis] = (pos[axis] + step) % 4
        return self.at(*pos, self.core)

    def other_core(self):
        return self.at(*self.pos, 1 - self.core)

    def greet(self):
        peers = [self.along(axis, step) for axis in range(3) for step in (1, 2, 3)]
        peers.append(self.other_core())
        barrier = pltpu.get_barrier_semaphore()
        for peer in peers:
            pl.semaphore_signal(barrier, inc=1, device_id=peer, device_id_type=MESH)
        pl.semaphore_wait(barrier, len(peers))

    def copy(self, src, dst, peer):
        out = pltpu.make_async_remote_copy(
            src_ref=src, dst_ref=dst, send_sem=self.send.at[self.used], recv_sem=self.recv.at[self.used],
            device_id=peer, device_id_type=MESH,
        )
        self.used += 1
        out.start()
        return out


def done(copies):
    for c in copies:
        c.wait()


def rows16(i, n=16):
    return pl.ds(pl.multiple_of(i * 16, 16), n)


class Gather:
    def __init__(self, links, x, full):
        self.links, self.full = links, full
        y = links.pos[1]
        across = links.g + 4 - 8 * (links.g // 4)
        own, self.other = rows16(links.g), rows16(across)
        self.column = [rows16(links.g - y + (y + 4 - d) % 4) for d in (1, 3, 2)]
        self.over = [links.copy(x.at[:, FIRST], full.at[own, FIRST], links.along(2, 2))]
        self.side = [links.copy(x.at[:, REST], full.at[own, REST], links.along(1, d)) for d in (1, 3, 2)]
        self.last = [links.copy(x.at[:, REST], full.at[own, REST], links.along(2, 2))]
        self.last += [links.copy(x.at[:, FIRST], full.at[own, FIRST], links.along(1, d)) for d in (1, 3, 2)]
        full[own, :] = x[...]

    def relay_over(self):
        done(self.over)
        part = self.full.at[self.other, FIRST]
        self.last += [self.links.copy(part, part, self.links.along(1, d)) for d in (1, 3, 2)]

    def relay_side(self):
        for c, rows in zip(self.side, self.column):
            c.wait()
            part = self.full.at[rows, REST]
            self.last.append(self.links.copy(part, part, self.links.along(2, 2)))

    def finish(self):
        done(self.last)


class Scatter:
    def __init__(self, links, part, out, near, far, send_far, last_far, pile, last_near):
        self.links, self.part, self.out = links, part, out
        self.near, self.far, self.send_far, self.last_far = near, far, send_far, last_far
        self.pile, self.last_near = pile, last_near
        y = links.pos[1]
        self.y = y
        self.here = links.g - y
        self.there = 4 - self.here
        self.a, self.b = [], []
        column = pl.ds(pl.multiple_of(self.there * 16, 16), 64)
        self.b.append(links.copy(part.at[column, REST], pile, links.along(2, 2)))
        for i, d in enumerate((1, 3, 2)):
            peer = (y + d) % 4
            for ref, base in ((far, self.there), (near, self.here)):
                self.a.append(links.copy(part.at[rows16(base + peer), FIRST], ref.at[i], links.along(1, d)))

    def middle(self):
        links, part, y = self.links, self.part, self.y
        done(self.a)
        total = part[rows16(self.there + y), FIRST].astype(F32)
        for i in range(3):
            total += self.far[i].astype(F32)
        self.send_far[...] = total.astype(BF)
        self.last = [links.copy(self.send_far, self.last_far, links.along(2, 2))]
        done(self.b)
        for i in range(4):
            rows = pl.ds(i * 16, 16)
            mine = part[rows16(self.here + i), REST].astype(F32)
            self.pile[rows, :] = (mine + self.pile[rows, :].astype(F32)).astype(BF)
        for i, d in enumerate((1, 3, 2)):
            self.last.append(links.copy(self.pile.at[rows16((y + d) % 4)], self.last_near.at[i], links.along(1, d)))

    def finish(self):
        done(self.last)
        total = self.part[rows16(self.here + self.y), FIRST].astype(F32) + self.last_far[...].astype(F32)
        for i in range(3):
            total += self.near[i].astype(F32)
        self.out[:, FIRST] = total.astype(BF)
        total = self.pile[rows16(self.y), :].astype(F32)
        for i in range(3):
            total += self.last_near[i].astype(F32)
        self.out[:, REST] = total.astype(BF)


def add_rows(dst, d0, srcs, n):
    step = 256 if n % 256 == 0 else n

    def body(t, _):
        total = None
        for ref, r in srcs:
            v = ref[pl.ds(pl.multiple_of(r + t * step, 16), step), :].astype(F32)
            total = v if total is None else total + v
        dst[pl.ds(pl.multiple_of(d0 + t * step, 16), step), :] = total.astype(BF)
        return 0

    if n == step:
        body(0, 0)
    else:
        lax.fori_loop(0, n // step, body, 0)


class SumAll:
    def __init__(self, links, g, inbox, slots, mid, small, full):
        self.links, self.g, self.slots, self.mid, self.small, self.full = links, g, slots, mid, small, full
        self.inbox = inbox
        self.home = links.core * HALF
        away = (1 - links.core) * HALF
        self.waiting, self.src, self.place, self.slot_at, at = {}, {}, {}, {}, 0
        for c, (base, size, axes) in enumerate(COLORS):
            self.src[c], self.place[c] = (g, self.home + base), self.home + base
            for s in range(3):
                self.slot_at[c, s] = at
                at += 3 * (size // 4 ** (s + 1))
            rows = pl.ds(pl.multiple_of(away + base, 16), size)
            self.waiting[c] = [links.copy(g.at[rows], inbox.at[pl.ds(base, size)], links.other_core())]

    def swapped(self, c):
        base, size, _ = COLORS[c]
        done(self.waiting[c])
        at = self.home + base
        add_rows(self.g, at, [(self.g, at), (self.inbox, base)], size)
        self.start(c, 0)

    def sizes(self, c, s):
        return COLORS[c][1] // 4 ** (s + 1), COLORS[c][2][s]

    def start(self, c, s):
        links = self.links
        (n, axis), (ref, row) = self.sizes(c, s), self.src[c]
        out = []
        for d in (1, 3, 2):
            j = (links.pos[axis] + d) % 4
            out.append(links.copy(
                ref.at[pl.ds(pl.multiple_of(row + j * n, 16), n)],
                self.slots.at[pl.ds(self.slot_at[c, s] + (d - 1) * n, n)],
                links.along(axis, d)))
        self.waiting[c] = out

    def reduce(self, c, s):
        (n, axis), (ref, row) = self.sizes(c, s), self.src[c]
        base = COLORS[c][0]
        own = row + self.links.pos[axis] * n
        self.place[c] = self.place[c] + self.links.pos[axis] * n
        done(self.waiting[c])
        srcs = [(ref, own)] + [(self.slots, self.slot_at[c, s] + d * n) for d in range(3)]
        dst, d0 = ((self.mid, base // 4), (self.small, base // 16), (self.full, self.place[c]))[s]
        add_rows(dst, d0, srcs, n)
        self.src[c] = (dst, d0)
        if s < 2:
            self.start(c, s + 1)
        else:
            self.share(c, 2)

    def share(self, c, s):
        n, axis = self.sizes(c, s)
        rows = self.full.at[pl.ds(pl.multiple_of(self.place[c], 16), n)]
        if s < 2:
            done(self.waiting[c])
        self.waiting[c] = [self.links.copy(rows, rows, self.links.along(axis, d)) for d in (1, 3, 2)]
        self.place[c] = self.place[c] - self.links.pos[axis] * n

    def back(self, c):
        done(self.waiting[c])
        rows = self.full.at[pl.ds(pl.multiple_of(self.place[c], 16), COLORS[c][1])]
        self.waiting[c] = [self.links.copy(rows, rows, self.links.other_core())]

    def each(self, step, *args):
        for c in range(N):
            step(c, *args)

    def finish(self):
        for c in range(N):
            done(self.waiting[c])


def layer_kernel(x, cx, src, tgt, cnt, wig, rad, w0, w1, w2, wg, agg, gn, full,
                 nodes, cot, w0t, w1t, w2t, wgt, wf, radt, ohs, oht, gbuf, R, mix, G, gate, gl, direct, bk,
                 pagg, near1, far1, send1, last1, pile1, lastn1, near2, far2, send2, last2, pile2, lastn2,
                 g, inbox, slots, mid, small, send, recv):
    links = Links(send, recv)
    links.greet()
    gather = Gather(links, x, nodes)
    prepare(src, tgt, cnt, wig, rad, wf, radt, ohs, oht)
    gather.relay_over()
    turn(w0, w0t)
    turn(w1.at[0], w1t.at[0])
    gather.relay_side()
    turn(w1.at[1], w1t.at[1])
    for i in range(2):
        turn(w2.at[i], w2t.at[i])
    turn(wg, wgt)
    gather.finish()
    gather = Gather(links, cx, cot)

    def hook(l):
        if l == 3:
            gather.relay_over()
        if l == 5:
            gather.relay_side()

    forward(nodes, wf, radt, ohs, w0t, w1t, w2t, wgt, gbuf, R, mix, gate, hook)
    gather.finish()
    low = backward(cot, wf, oht, wg, gbuf, mix, gate, G, gl, direct)
    weight_grads(R, G, mix, low, g)
    total = SumAll(links, g, inbox, slots, mid, small, full)

    def hook(l):
        if l == 4:
            total.each(total.swapped)

    send_messages(wf, mix, gate, oht, bk, pagg, hook)
    first = Scatter(links, pagg, agg, near1, far1, send1, last1, pile1, lastn1)
    rotated_grads(radt, w0, w1, w2, G, R)

    def hook(l):
        if l == 4:
            total.each(total.reduce, 0)
            first.middle()
        if l == 5:
            total.each(total.reduce, 1)

    source_grads(wf, ohs, R, bk, nodes, hook)
    second = Scatter(links, nodes, gn, near2, far2, send2, last2, pile2, lastn2)
    total.each(total.reduce, 2)
    total.each(total.share, 1)
    first.finish()
    total.each(total.share, 0)
    second.middle()
    total.each(total.back)
    second.finish()
    total.finish()


def unpack_kernel(full, agg, gn, agg_o, gn_o, zero, one, two, last, buf, b0, b1, b2, b3, s_in, s_out):
    pieces = [(full.at[pl.ds(lo, hi - lo)], buf.at[pl.ds(lo, hi - lo)]) for lo, hi in zip(BOUNDS[:-1], BOUNDS[1:])]
    loads = [pltpu.make_async_copy(a, b, s_in.at[i]) for i, (a, b) in enumerate(pieces)]
    for c in loads:
        c.start()
    stores = [pltpu.make_async_copy(agg, agg_o, s_out.at[6]), pltpu.make_async_copy(gn, gn_o, s_out.at[7])]
    for c in stores:
        c.start()
    targets = [(b0, zero), (b1.at[0], one.at[0]), (b1.at[1], one.at[1]), (b2.at[0], two.at[0]), (b2.at[1], two.at[1]), (b3, last)]
    for i, (tile, out) in enumerate(targets):
        loads[i].wait()
        n = tile.shape[0]
        for p in range(n // 128):
            at = BOUNDS[i] + p * n
            tile[:, p * 128 : (p + 1) * 128] = buf[at : at + n, :].astype(F32)
        stores.append(pltpu.make_async_copy(tile, out, s_out.at[i]))
        stores[-1].start()
    for c in stores:
        c.wait()


BOUNDS = (0, ONE_AT, ONE_AT + 4608, TWO_AT, TWO_AT + 3200, GATE_AT, USED)


def scatter_scratch():
    first, rest = CUT, 6272 - CUT
    shapes = ((3, 16, first), (3, 16, first), (16, first), (16, first), (64, rest), (3, 16, rest))
    return [pltpu.VMEM(shape, BF) for shape in shapes]


def per_device(nodes, sources, targets, counts, wigner, radial, cotangent, w0, w1, w2, wg):
    vm = pl.BlockSpec(memory_space=pltpu.VMEM)
    hbm = pl.BlockSpec(memory_space=pl.ANY)
    dma = pltpu.SemaphoreType.DMA
    agg, gn, full = pl.pallas_call(
        layer_kernel,
        out_shape=(
            jax.ShapeDtypeStruct((16, 6272), BF),
            jax.ShapeDtypeStruct((16, 6272), BF),
            jax.ShapeDtypeStruct((TOTAL, 128), BF),
        ),
        in_specs=[vm] * 11,
        out_specs=(vm, vm, vm),
        scratch_shapes=[
            pltpu.VMEM((128, 6272), BF),
            pltpu.VMEM((128, 6272), BF),
            pltpu.VMEM((896, 896), BF),
            pltpu.VMEM((2, 768, 768), BF),
            pltpu.VMEM((2, 640, 640), BF),
            pltpu.VMEM((128, 128), BF),
            pltpu.VMEM((4, 49, 32, 128), F32),
            pltpu.VMEM((128, 512), F32),
            pltpu.VMEM((128, 512), BF),
            pltpu.VMEM((128, 512), BF),
            pltpu.VMEM((13 * 128, 512), BF),
            pltpu.VMEM((3712, 512), BF),
            pltpu.VMEM((3712, 512), F32),
            pltpu.VMEM((3712, 512), BF),
            pltpu.VMEM((128, 512), F32),
            pltpu.VMEM((128, 512), F32),
            pltpu.VMEM((128, 512), F32),
            pltpu.VMEM((13 * 128, 512), BF),
            pltpu.VMEM((128, 6272), BF),
            *scatter_scratch(),
            *scatter_scratch(),
            pltpu.VMEM((TOTAL, 128), BF),
            pltpu.VMEM((HALF, 128), BF),
            pltpu.VMEM((SLOT_ROWS, 128), BF),
            pltpu.VMEM((HALF // 4, 128), BF),
            pltpu.VMEM((HALF // 16, 128), BF),
            dma((N_SEMS,)),
            dma((N_SEMS,)),
        ],
        compiler_params=pltpu.CompilerParams(
            vmem_limit_bytes=67043328, collective_id=0, has_side_effects=True
        ),
        name="edge_layer",
    )(nodes[0], cotangent[0], sources, targets, counts, jnp.swapaxes(wigner[0], 0, 1), radial[0], w0, w1, w2, wg)
    return_shapes = [(16, 6272)] * 2 + [(896, 896), (2, 768, 768), (2, 640, 640), (128, 128)]
    agg, gn, zero, one, two, last = pl.pallas_call(
        unpack_kernel,
        out_shape=[jax.ShapeDtypeStruct(shape, BF if i < 2 else F32) for i, shape in enumerate(return_shapes)],
        in_specs=[hbm, vm, vm],
        out_specs=[hbm] * 6,
        scratch_shapes=[
            pltpu.VMEM((USED, 128), BF),
            *[pltpu.VMEM(shape, F32) for shape in return_shapes[2:]],
            dma((6,)),
            dma((8,)),
        ],
        compiler_params=pltpu.CompilerParams(vmem_limit_bytes=67043328),
        name="unpack",
    )(full, agg, gn)
    return agg[None], gn[None], zero, one, two, last


def solution(mesh):
    in_specs = (
        P("dp", "graph", None),
        P("dp", "graph"),
        P("dp", "graph"),
        P("dp", "graph"),
        P("dp", None, None, "graph"),
        P("dp", "graph", None),
        P("dp", "graph", None),
        P(),
        P(),
        P(),
        P(),
    )
    out_specs = (P("dp", "graph", None), P("dp", "graph", None), P(), P(), P(), P())
    return jax.shard_map(
        per_device, mesh=mesh, in_specs=in_specs, out_specs=out_specs, check_vma=False
    )
```

```python
import jax
import jax.numpy as jnp
from jax import lax
from jax.experimental import pallas as pl
from jax.experimental.pallas import tpu as pltpu
from jax.sharding import PartitionSpec as P

BF = jnp.bfloat16
F32 = jnp.float32
C = 128
CH = 32
ONE_AT, TWO_AT, GATE_AT, USED, TOTAL = 6272, 15488, 21888, 22016, 22528


def kept(l):
    ks = [l]
    if l >= 1:
        ks += [7 + l - 1, 13 + l - 1]
    if l >= 2:
        ks += [19 + l - 2, 24 + l - 2]
    return ks


def nn(a, b):
    return jnp.dot(a, b, preferred_element_type=F32)


def nt(a, b):
    return lax.dot_general(a, b, (((1,), (1,)), ((), ())), preferred_element_type=F32)


def tn(a, b):
    return lax.dot_general(a, b, (((0,), (0,)), ((), ())), preferred_element_type=F32)


def weighted(terms):
    total = None
    for w, v in terms:
        part = v.reshape(CH // 8, 8, 128) * w[None]
        total = part if total is None else total + part
    return total.reshape(CH, 128)


def prepare(src, tgt, cnt, wig, rad, wf, radt, ohs, oht):
    edges = src.shape[1]

    def spread_row(j, _):
        for q in range(4):
            wf[q, j, 0:29, :] = wig[j, :, q * 128 : (q + 1) * 128].astype(F32)
        return 0

    lax.fori_loop(0, 49, spread_row, 0)
    node = lax.broadcasted_iota(jnp.int32, (128, edges), 0)
    slot = lax.broadcasted_iota(jnp.int32, (128, edges), 1)
    ohs[...] = jnp.where(node == src[...], 1.0, 0.0).astype(BF)
    live = slot < cnt[...]
    oht[...] = jnp.where((node == tgt[...]) & live, 1.0, 0.0).astype(BF)
    radt[...] = rad[...].astype(F32).T


def turn(block, out):
    def step(i, _):
        at = pl.multiple_of(i * 128, 128)
        out[:, pl.ds(at, 128)] = block[pl.ds(at, 128), :].T
        return 0

    lax.fori_loop(0, block.shape[0] // 128, step, 0)


INTERPRET = False


def row(wf, q, k, j):
    if INTERPRET:
        return jnp.broadcast_to(wf[q, j, pl.ds(k, 1), :], (8, 128))
    return wf[q, j, pl.ds(k, 8, stride=0), :]


def tiles(body):
    def step(t, _):
        body(pl.multiple_of((t // 4) * CH, CH), t % 4)
        return 0

    lax.fori_loop(0, 4 * (128 // CH), step, 0)


def turn_in(l, wf, gbuf, emit):
    count = 2 * l + 1

    def body(c0, q):
        e0 = pl.multiple_of(q * 128, 128)
        vals = [gbuf[pl.ds(j * 128 + c0, CH), pl.ds(e0, 128)].astype(F32) for j in range(count)]
        for k in kept(l):
            emit(k, weighted([(row(wf, q, k, l * l + j), vals[j]) for j in range(count)]), c0, e0)

    tiles(body)


def turn_out(l, wf, load, bk):
    count = 2 * l + 1

    def body(c0, q):
        e0 = pl.multiple_of(q * 128, 128)
        vals = [load(k, c0, e0) for k in kept(l)]
        for j in range(count):
            out = weighted([(row(wf, q, k, l * l + j), v) for k, v in zip(kept(l), vals)])
            bk[pl.ds(j * 128 + c0, CH), pl.ds(e0, 128)] = out.astype(BF)

    tiles(body)


def halves(body):
    def step(h, _):
        body(pl.ds(pl.multiple_of(h * 256, 256), 256))
        return 0

    lax.fori_loop(0, 2, step, 0)


def sigmoid(v):
    return 1.0 / (1.0 + jnp.exp(-v))


def cols(l):
    return slice(l * l * 128, (l + 1) * (l + 1) * 128)


def forward(nodes, wf, radt, ohs, w0t, w1t, w2t, wgt, gbuf, R, mix, gate, hook):
    for l in range(7):
        gbuf[0 : (2 * l + 1) * 128, :] = tn(nodes[:, cols(l)], ohs[...]).astype(BF)

        def emit(k, v, c0, e0):
            R[pl.ds(k * 128 + c0, CH), pl.ds(e0, 128)] = (v * radt[pl.ds(c0, CH), pl.ds(e0, 128)]).astype(BF)

        turn_in(l, wf, gbuf, emit)
        hook(l)

    def zero(e):
        mix[0:896, e] = nn(w0t[...], R[0:896, e])
        scalar = mix[0:128, e].astype(BF)
        gate[:, e] = sigmoid(nn(wgt[...], scalar))

    halves(zero)
    for wt, at, n in ((w1t, 896, 768), (w2t, 2432, 640)):
        def pair(e):
            p, m = R[at : at + n, e], R[at + n : at + 2 * n, e]
            mix[at : at + n, e] = nn(wt[0], p) - nn(wt[1], m)
            mix[at + n : at + 2 * n, e] = nn(wt[1], p) + nn(wt[0], m)

        halves(pair)


def send_messages(wf, mix, gate, oht, bk, agg, hook):
    for l in range(7):
        def load(k, c0, e0):
            v = mix[pl.ds(k * 128 + c0, CH), pl.ds(e0, 128)]
            m = v * sigmoid(v) if k == 0 else v * gate[pl.ds(c0, CH), pl.ds(e0, 128)]
            return m.astype(BF).astype(F32)

        turn_out(l, wf, load, bk)
        agg[:, cols(l)] = nt(oht[...], bk[0 : (2 * l + 1) * 128, :]).astype(BF)
        hook(l)


def backward(cot, wf, oht, wg, gbuf, mix, gate, G, gl, direct):
    gl[...] = jnp.zeros_like(gl)
    for l in range(7):
        gbuf[0 : (2 * l + 1) * 128, :] = tn(cot[:, cols(l)], oht[...]).astype(BF)

        def emit(k, v, c0, e0):
            at = (pl.ds(c0, CH), pl.ds(e0, 128))
            x = mix[pl.ds(k * 128 + c0, CH), pl.ds(e0, 128)]
            if k == 0:
                s = sigmoid(x)
                direct[at] = v * s * (1.0 + x * (1.0 - s))
            else:
                G[pl.ds(k * 128 + c0, CH), pl.ds(e0, 128)] = (v * gate[at]).astype(BF)
                gl[at] += v * x

        turn_in(l, wf, gbuf, emit)
    low = (gl[...] * gate[...] * (1.0 - gate[...])).astype(BF)
    G[0:128, :] = (direct[...] + nn(wg[...], low)).astype(BF)
    return low


def weight_grads(R, G, mix, low, g):
    for at in (0, 256, 512, 768):
        wide = min(256, 896 - at)
        out = nt(R[0:896, :], G[at : at + wide, :]).astype(BF)
        for q in range(wide // 128):
            p = at // 128 + q
            g[p * 896 : (p + 1) * 896, :] = out[:, q * 128 : (q + 1) * 128]
    for base, at, n in ((ONE_AT, 896, 768), (TWO_AT, 2432, 640)):
        for lo in range(0, n, 256):
            wide = min(256, n - lo)
            plus, minus = G[at + lo : at + lo + wide, :], G[at + n + lo : at + n + lo + wide, :]
            rp, rm = R[at : at + n, :], R[at + n : at + 2 * n, :]
            for i, out in enumerate((nt(rp, plus) + nt(rm, minus), nt(rp, minus) - nt(rm, plus))):
                out = out.astype(BF)
                for q in range(wide // 128):
                    r = base + (i * (n // 128) + lo // 128 + q) * n
                    g[r : r + n, :] = out[:, q * 128 : (q + 1) * 128]
    g[GATE_AT:USED, :] = nt(mix[0:128, :].astype(BF), low).astype(BF)
    g[USED:TOTAL, :] = jnp.zeros((TOTAL - USED, 128), BF)


def rotated_grads(radt, w0, w1, w2, G, R):
    def scale(v, e):
        n = v.shape[0]
        return (v.reshape(n // 128, 128, v.shape[1]) * radt[:, e][None]).reshape(v.shape).astype(BF)

    def zero(e):
        R[0:896, e] = scale(nn(w0[...], G[0:896, e]), e)

    halves(zero)
    for w, at, n in ((w1, 896, 768), (w2, 2432, 640)):
        def pair(e):
            p, m = G[at : at + n, e], G[at + n : at + 2 * n, e]
            R[at : at + n, e] = scale(nn(w[0], p) + nn(w[1], m), e)
            R[at + n : at + 2 * n, e] = scale(nn(w[0], m) - nn(w[1], p), e)

        halves(pair)


def source_grads(wf, ohs, R, bk, gn, hook):
    for l in range(7):
        def load(k, c0, e0):
            return R[pl.ds(k * 128 + c0, CH), pl.ds(e0, 128)].astype(F32)

        turn_out(l, wf, load, bk)
        gn[:, cols(l)] = nt(ohs[...], bk[0 : (2 * l + 1) * 128, :]).astype(BF)
        hook(l)


HALF = TOTAL // 2
MESH = pl.DeviceIdType.MESH
CUT = 24 * 128
FIRST, REST = slice(0, CUT), slice(CUT, 6272)
COLORS = (
    (0, 2048, (0, 1, 2)),
    (2048, 2048, (1, 2, 0)),
    (4096, 2048, (2, 0, 1)),
    (6144, 2048, (0, 2, 1)),
    (8192, 2048, (1, 0, 2)),
    (10240, 1024, (2, 1, 0)),
)
EARLY, LATE, ALL = (0, 1, 2), (3, 4, 5), (0, 1, 2, 3, 4, 5)
N = len(COLORS)
SLOT_ROWS = sum(3 * (size // 4 + size // 16 + size // 64) for _, size, _ in COLORS)
N_SEMS = 2 * 14 + 2 * 11 + 5 * N + 2 * 9 * N
N_SEND = 56


class Links:
    def __init__(self, send, recv):
        dp, self.g = lax.axis_index("dp"), lax.axis_index("graph")
        self.dp = dp
        self.pos = (dp // 4, self.g % 4, (self.g // 4) * 2 + (dp // 2) % 2)
        self.core = dp % 2
        self.send, self.recv, self.used = send, recv, 0
        self.free = list(range(N_SEND - 1, -1, -1))

    def at(self, x, y, z, core):
        return ((x * 2 + z % 2) * 2 + core, (z // 2) * 4 + y)

    def along(self, axis, step):
        pos = list(self.pos)
        pos[axis] = (pos[axis] + step) % 4
        return self.at(*pos, self.core)

    def other_core(self):
        return self.at(*self.pos, 1 - self.core)

    def greet(self):
        peers = [self.along(axis, step) for axis in range(3) for step in (1, 2, 3)]
        peers.append(self.other_core())
        barrier = pltpu.get_barrier_semaphore()
        for peer in peers:
            pl.semaphore_signal(barrier, inc=1, device_id=peer, device_id_type=MESH)
        pl.semaphore_wait(barrier, len(peers))

    def copy(self, src, dst, peer):
        slot = self.free.pop()
        out = pltpu.make_async_remote_copy(
            src_ref=src, dst_ref=dst, send_sem=self.send.at[slot], recv_sem=self.recv.at[self.used],
            device_id=peer, device_id_type=MESH,
        )
        self.used += 1
        out.start()
        return Sent(self, out, slot)


class Sent:
    def __init__(self, links, out, slot):
        self.links, self.out, self.slot = links, out, slot

    def wait(self):
        self.out.wait()
        self.links.free.append(self.slot)


def done(copies):
    for c in copies:
        c.wait()


def rows16(i, n=16):
    return pl.ds(pl.multiple_of(i * 16, 16), n)


class Gather:
    def __init__(self, links, x, full):
        self.links, self.full = links, full
        y = links.pos[1]
        across = links.g + 4 - 8 * (links.g // 4)
        own, self.other = rows16(links.g), rows16(across)
        self.column = [rows16(links.g - y + (y + 4 - d) % 4) for d in (1, 3, 2)]
        self.over = [links.copy(x.at[:, FIRST], full.at[own, FIRST], links.along(2, 2))]
        self.side = [links.copy(x.at[:, REST], full.at[own, REST], links.along(1, d)) for d in (1, 3, 2)]
        self.last = [links.copy(x.at[:, REST], full.at[own, REST], links.along(2, 2))]
        self.last += [links.copy(x.at[:, FIRST], full.at[own, FIRST], links.along(1, d)) for d in (1, 3, 2)]
        full[own, :] = x[...]

    def relay_over(self):
        done(self.over)
        part = self.full.at[self.other, FIRST]
        self.last += [self.links.copy(part, part, self.links.along(1, d)) for d in (1, 3, 2)]

    def relay_side(self):
        for c, rows in zip(self.side, self.column):
            c.wait()
            part = self.full.at[rows, REST]
            self.last.append(self.links.copy(part, part, self.links.along(2, 2)))

    def finish(self):
        done(self.last)


class Scatter:
    def __init__(self, links, part, out, near, far, send_far, last_far, pile, last_near):
        self.links, self.part, self.out = links, part, out
        self.near, self.far, self.send_far, self.last_far = near, far, send_far, last_far
        self.pile, self.last_near = pile, last_near
        y = links.pos[1]
        self.y = y
        self.here = links.g - y
        self.there = 4 - self.here
        self.a, self.b = [], []
        column = pl.ds(pl.multiple_of(self.there * 16, 16), 64)
        self.b.append(links.copy(part.at[column, REST], pile, links.along(2, 2)))
        for i, d in enumerate((1, 3, 2)):
            peer = (y + d) % 4
            for ref, base in ((far, self.there), (near, self.here)):
                self.a.append(links.copy(part.at[rows16(base + peer), FIRST], ref.at[i], links.along(1, d)))

    def middle(self):
        links, part, y = self.links, self.part, self.y
        done(self.a)
        total = part[rows16(self.there + y), FIRST].astype(F32)
        for i in range(3):
            total += self.far[i].astype(F32)
        self.send_far[...] = total.astype(BF)
        self.last = [links.copy(self.send_far, self.last_far, links.along(2, 2))]
        done(self.b)
        for i in range(4):
            rows = pl.ds(i * 16, 16)
            mine = part[rows16(self.here + i), REST].astype(F32)
            self.pile[rows, :] = (mine + self.pile[rows, :].astype(F32)).astype(BF)
        for i, d in enumerate((1, 3, 2)):
            self.last.append(links.copy(self.pile.at[rows16((y + d) % 4)], self.last_near.at[i], links.along(1, d)))

    def finish(self):
        done(self.last)
        total = self.part[rows16(self.here + self.y), FIRST].astype(F32) + self.last_far[...].astype(F32)
        for i in range(3):
            total += self.near[i].astype(F32)
        self.out[:, FIRST] = total.astype(BF)
        total = self.pile[rows16(self.y), :].astype(F32)
        for i in range(3):
            total += self.last_near[i].astype(F32)
        self.out[:, REST] = total.astype(BF)


def add_rows(dst, d0, srcs, n):
    step = 256 if n % 256 == 0 else n

    def body(t, _):
        total = None
        for ref, r in srcs:
            v = ref[pl.ds(pl.multiple_of(r + t * step, 16), step), :].astype(F32)
            total = v if total is None else total + v
        dst[pl.ds(pl.multiple_of(d0 + t * step, 16), step), :] = total.astype(BF)
        return 0

    if n == step:
        body(0, 0)
    else:
        lax.fori_loop(0, n // step, body, 0)


class SumAll:
    def __init__(self, links, g, inbox, slots, mid, small, full):
        self.links, self.g, self.slots, self.mid, self.small, self.full = links, g, slots, mid, small, full
        self.inbox, self.swaps = inbox, []
        self.home = links.core * HALF
        away = (1 - links.core) * HALF
        self.waiting, self.src, self.place, self.slot_at, at = {}, {}, {}, {}, 0
        for c, (base, size, axes) in enumerate(COLORS):
            self.src[c], self.place[c] = (g, self.home + base), self.home + base
            for s in range(3):
                self.slot_at[c, s] = at
                at += 3 * (size // 4 ** (s + 1))
            rows = pl.ds(pl.multiple_of(away + base, 16), size)
            self.waiting[c] = [links.copy(g.at[rows], inbox.at[pl.ds(base, size)], links.other_core())]

    def swapped(self, c):
        base, size, _ = COLORS[c]
        done(self.waiting[c])
        at = self.home + base
        add_rows(self.g, at, [(self.g, at), (self.inbox, base)], size)

    def sizes(self, c, s):
        return COLORS[c][1] // 4 ** (s + 1), COLORS[c][2][s]

    def start(self, c, s):
        links = self.links
        (n, axis), (ref, row) = self.sizes(c, s), self.src[c]
        out = []
        for d in (1, 3, 2):
            j = (links.pos[axis] + d) % 4
            out.append(links.copy(
                ref.at[pl.ds(pl.multiple_of(row + j * n, 16), n)],
                self.slots.at[pl.ds(self.slot_at[c, s] + (d - 1) * n, n)],
                links.along(axis, d)))
        self.waiting[c] = out

    def reduce(self, c, s):
        (n, axis), (ref, row) = self.sizes(c, s), self.src[c]
        base = COLORS[c][0]
        own = row + self.links.pos[axis] * n
        self.place[c] = self.place[c] + self.links.pos[axis] * n
        done(self.waiting[c])
        srcs = [(ref, own)] + [(self.slots, self.slot_at[c, s] + d * n) for d in range(3)]
        dst, d0 = ((self.mid, base // 4), (self.small, base // 16), (self.full, self.place[c]))[s]
        add_rows(dst, d0, srcs, n)
        self.src[c] = (dst, d0)
        if s < 2:
            self.start(c, s + 1)
        else:
            self.share(c, 2)

    def share(self, c, s):
        n, axis = self.sizes(c, s)
        rows = self.full.at[pl.ds(pl.multiple_of(self.place[c], 16), n)]
        if s < 2:
            done(self.waiting[c])
        self.waiting[c] = [self.links.copy(rows, rows, self.links.along(axis, d)) for d in (1, 3, 2)]
        if s == 0:
            self.swaps.append(self.links.copy(rows, rows, self.links.other_core()))
        self.place[c] = self.place[c] - self.links.pos[axis] * n

    def back(self, c):
        n, axis = self.sizes(c, 0)
        for copy, d in zip(self.waiting[c], (1, 3, 2)):
            copy.wait()
            block = (self.links.pos[axis] + 4 - d) % 4
            rows = self.full.at[pl.ds(pl.multiple_of(self.place[c] + block * n, 16), n)]
            self.swaps.append(self.links.copy(rows, rows, self.links.other_core()))

    def finish(self):
        done(self.swaps)

    def each(self, colors, step, *args):
        for c in colors:
            step(c, *args)


def layer_kernel(x, cx, src, tgt, cnt, wig, rad, w0, w1, w2, wg, agg, gn, full,
                 nodes, cot, w0t, w1t, w2t, wgt, wf, radt, ohs, oht, gbuf, R, mix, G, gate, gl, direct, bk,
                 pagg, near1, far1, send1, last1, pile1, lastn1, near2, far2, send2, last2, pile2, lastn2,
                 g, inbox, slots, mid, small, send, recv):
    links = Links(send, recv)
    links.greet()
    gather = Gather(links, x, nodes)
    prepare(src, tgt, cnt, wig, rad, wf, radt, ohs, oht)
    gather.relay_over()
    turn(w0, w0t)
    turn(w1.at[0], w1t.at[0])
    gather.relay_side()
    turn(w1.at[1], w1t.at[1])
    for i in range(2):
        turn(w2.at[i], w2t.at[i])
    turn(wg, wgt)
    gather.finish()
    gather = Gather(links, cx, cot)

    def hook(l):
        if l == 3:
            gather.relay_over()
        if l == 5:
            gather.relay_side()

    forward(nodes, wf, radt, ohs, w0t, w1t, w2t, wgt, gbuf, R, mix, gate, hook)
    gather.finish()
    low = backward(cot, wf, oht, wg, gbuf, mix, gate, G, gl, direct)
    weight_grads(R, G, mix, low, g)
    total = SumAll(links, g, inbox, slots, mid, small, full)

    def hook(l):
        colors = {3: EARLY, 5: LATE}.get(l, ())
        total.each(colors, total.swapped)
        total.each(colors, total.start, 0)

    send_messages(wf, mix, gate, oht, bk, pagg, hook)
    first = Scatter(links, pagg, agg, near1, far1, send1, last1, pile1, lastn1)
    rotated_grads(radt, w0, w1, w2, G, R)

    def hook(l):
        if l == 2:
            total.each(EARLY, total.reduce, 0)
        if l == 4:
            total.each(LATE, total.reduce, 0)
            first.middle()
        if l == 5:
            total.each(ALL, total.reduce, 1)

    source_grads(wf, ohs, R, bk, nodes, hook)
    second = Scatter(links, nodes, gn, near2, far2, send2, last2, pile2, lastn2)
    total.each(ALL, total.reduce, 2)
    total.each(ALL, total.share, 1)
    first.finish()
    total.each(ALL, total.share, 0)
    second.middle()
    total.each(ALL, total.back)
    second.finish()
    total.finish()


def unpack_kernel(full, agg, gn, agg_o, gn_o, zero, one, two, last, buf, b0, b1, b2, b3, s_in, s_out):
    pieces = [(full.at[pl.ds(lo, hi - lo)], buf.at[pl.ds(lo, hi - lo)]) for lo, hi in zip(BOUNDS[:-1], BOUNDS[1:])]
    loads = [pltpu.make_async_copy(a, b, s_in.at[i]) for i, (a, b) in enumerate(pieces)]
    for c in loads:
        c.start()
    stores = [pltpu.make_async_copy(agg, agg_o, s_out.at[6]), pltpu.make_async_copy(gn, gn_o, s_out.at[7])]
    for c in stores:
        c.start()
    targets = [(b0, zero), (b1.at[0], one.at[0]), (b1.at[1], one.at[1]), (b2.at[0], two.at[0]), (b2.at[1], two.at[1]), (b3, last)]
    for i, (tile, out) in enumerate(targets):
        loads[i].wait()
        n = tile.shape[0]
        for p in range(n // 128):
            at = BOUNDS[i] + p * n
            tile[:, p * 128 : (p + 1) * 128] = buf[at : at + n, :].astype(F32)
        stores.append(pltpu.make_async_copy(tile, out, s_out.at[i]))
        stores[-1].start()
    for c in stores:
        c.wait()


BOUNDS = (0, ONE_AT, ONE_AT + 4608, TWO_AT, TWO_AT + 3200, GATE_AT, USED)


def scatter_scratch():
    first, rest = CUT, 6272 - CUT
    shapes = ((3, 16, first), (3, 16, first), (16, first), (16, first), (64, rest), (3, 16, rest))
    return [pltpu.VMEM(shape, BF) for shape in shapes]


def per_device(nodes, sources, targets, counts, wigner, radial, cotangent, w0, w1, w2, wg):
    vm = pl.BlockSpec(memory_space=pltpu.VMEM)
    hbm = pl.BlockSpec(memory_space=pl.ANY)
    dma = pltpu.SemaphoreType.DMA
    agg, gn, full = pl.pallas_call(
        layer_kernel,
        out_shape=(
            jax.ShapeDtypeStruct((16, 6272), BF),
            jax.ShapeDtypeStruct((16, 6272), BF),
            jax.ShapeDtypeStruct((TOTAL, 128), BF),
        ),
        in_specs=[vm] * 11,
        out_specs=(vm, vm, vm),
        scratch_shapes=[
            pltpu.VMEM((128, 6272), BF),
            pltpu.VMEM((128, 6272), BF),
            pltpu.VMEM((896, 896), BF),
            pltpu.VMEM((2, 768, 768), BF),
            pltpu.VMEM((2, 640, 640), BF),
            pltpu.VMEM((128, 128), BF),
            pltpu.VMEM((4, 49, 32, 128), F32),
            pltpu.VMEM((128, 512), F32),
            pltpu.VMEM((128, 512), BF),
            pltpu.VMEM((128, 512), BF),
            pltpu.VMEM((13 * 128, 512), BF),
            pltpu.VMEM((3712, 512), BF),
            pltpu.VMEM((3712, 512), F32),
            pltpu.VMEM((3712, 512), BF),
            pltpu.VMEM((128, 512), F32),
            pltpu.VMEM((128, 512), F32),
            pltpu.VMEM((128, 512), F32),
            pltpu.VMEM((13 * 128, 512), BF),
            pltpu.VMEM((128, 6272), BF),
            *scatter_scratch(),
            *scatter_scratch(),
            pltpu.VMEM((TOTAL, 128), BF),
            pltpu.VMEM((HALF, 128), BF),
            pltpu.VMEM((SLOT_ROWS, 128), BF),
            pltpu.VMEM((HALF // 4, 128), BF),
            pltpu.VMEM((HALF // 16, 128), BF),
            dma((N_SEND,)),
            dma((N_SEMS,)),
        ],
        compiler_params=pltpu.CompilerParams(
            vmem_limit_bytes=67043328, collective_id=0, has_side_effects=True
        ),
        name="edge_layer",
    )(nodes[0], cotangent[0], sources, targets, counts, jnp.swapaxes(wigner[0], 0, 1), radial[0], w0, w1, w2, wg)
    return_shapes = [(16, 6272)] * 2 + [(896, 896), (2, 768, 768), (2, 640, 640), (128, 128)]
    agg, gn, zero, one, two, last = pl.pallas_call(
        unpack_kernel,
        out_shape=[jax.ShapeDtypeStruct(shape, BF if i < 2 else F32) for i, shape in enumerate(return_shapes)],
        in_specs=[hbm, vm, vm],
        out_specs=[hbm] * 6,
        scratch_shapes=[
            pltpu.VMEM((USED, 128), BF),
            *[pltpu.VMEM(shape, F32) for shape in return_shapes[2:]],
            dma((6,)),
            dma((8,)),
        ],
        compiler_params=pltpu.CompilerParams(vmem_limit_bytes=67043328),
        name="unpack",
    )(full, agg, gn)
    return agg[None], gn[None], zero, one, two, last


def solution(mesh):
    in_specs = (
        P("dp", "graph", None),
        P("dp", "graph"),
        P("dp", "graph"),
        P("dp", "graph"),
        P("dp", None, None, "graph"),
        P("dp", "graph", None),
        P("dp", "graph", None),
        P(),
        P(),
        P(),
        P(),
    )
    out_specs = (P("dp", "graph", None), P("dp", "graph", None), P(), P(), P(), P())
    return jax.shard_map(
        per_device, mesh=mesh, in_specs=in_specs, out_specs=out_specs, check_vma=False
    )
```

```python
import jax
import jax.numpy as jnp
from jax import lax
from jax.experimental import pallas as pl
from jax.experimental.pallas import tpu as pltpu
from jax.sharding import PartitionSpec as P

BF = jnp.bfloat16
F32 = jnp.float32
C = 128
CH = 32
ONE_AT, TWO_AT, GATE_AT, USED, TOTAL = 6272, 15488, 21888, 22016, 22528


def kept(l):
    ks = [l]
    if l >= 1:
        ks += [7 + l - 1, 13 + l - 1]
    if l >= 2:
        ks += [19 + l - 2, 24 + l - 2]
    return ks


def nn(a, b):
    return jnp.dot(a, b, preferred_element_type=F32)


def nt(a, b):
    return lax.dot_general(a, b, (((1,), (1,)), ((), ())), preferred_element_type=F32)


def tn(a, b):
    return lax.dot_general(a, b, (((0,), (0,)), ((), ())), preferred_element_type=F32)


def weighted(terms):
    total = None
    for w, v in terms:
        part = v.reshape(CH // 8, 8, 128) * w[None]
        total = part if total is None else total + part
    return total.reshape(CH, 128)


def prepare(src, tgt, cnt, wig, rad, wf, radt, ohs, oht):
    edges = src.shape[1]

    def spread_row(j, _):
        for q in range(4):
            wf[q, j, 0:29, :] = wig[j, :, q * 128 : (q + 1) * 128].astype(F32)
        return 0

    lax.fori_loop(0, 49, spread_row, 0)
    node = lax.broadcasted_iota(jnp.int32, (128, edges), 0)
    slot = lax.broadcasted_iota(jnp.int32, (128, edges), 1)
    ohs[...] = jnp.where(node == src[...], 1.0, 0.0).astype(BF)
    live = slot < cnt[...]
    oht[...] = jnp.where((node == tgt[...]) & live, 1.0, 0.0).astype(BF)
    radt[...] = rad[...].astype(F32).T


def turn(block, out):
    def step(i, _):
        at = pl.multiple_of(i * 128, 128)
        out[:, pl.ds(at, 128)] = block[pl.ds(at, 128), :].T
        return 0

    lax.fori_loop(0, block.shape[0] // 128, step, 0)


INTERPRET = False


def row(wf, q, k, j):
    if INTERPRET:
        return jnp.broadcast_to(wf[q, j, pl.ds(k, 1), :], (8, 128))
    return wf[q, j, pl.ds(k, 8, stride=0), :]


def tiles(body):
    def step(t, _):
        body(pl.multiple_of((t // 4) * CH, CH), t % 4)
        return 0

    lax.fori_loop(0, 4 * (128 // CH), step, 0)


def turn_in(l, wf, gbuf, emit):
    count = 2 * l + 1

    def body(c0, q):
        e0 = pl.multiple_of(q * 128, 128)
        vals = [gbuf[pl.ds(j * 128 + c0, CH), pl.ds(e0, 128)].astype(F32) for j in range(count)]
        for k in kept(l):
            emit(k, weighted([(row(wf, q, k, l * l + j), vals[j]) for j in range(count)]), c0, e0)

    tiles(body)


def turn_out(l, wf, load, bk):
    count = 2 * l + 1

    def body(c0, q):
        e0 = pl.multiple_of(q * 128, 128)
        vals = [load(k, c0, e0) for k in kept(l)]
        for j in range(count):
            out = weighted([(row(wf, q, k, l * l + j), v) for k, v in zip(kept(l), vals)])
            bk[pl.ds(j * 128 + c0, CH), pl.ds(e0, 128)] = out.astype(BF)

    tiles(body)


def halves(body):
    def step(h, _):
        body(pl.ds(pl.multiple_of(h * 256, 256), 256))
        return 0

    lax.fori_loop(0, 2, step, 0)


def sigmoid(v):
    return 1.0 / (1.0 + jnp.exp(-v))


def cols(l):
    return slice(l * l * 128, (l + 1) * (l + 1) * 128)


def forward(nodes, wf, radt, ohs, w0t, w1t, w2t, wgt, gbuf, R, mix, gate, hook):
    for l in range(7):
        gbuf[0 : (2 * l + 1) * 128, :] = tn(nodes[:, cols(l)], ohs[...]).astype(BF)

        def emit(k, v, c0, e0):
            R[pl.ds(k * 128 + c0, CH), pl.ds(e0, 128)] = (v * radt[pl.ds(c0, CH), pl.ds(e0, 128)]).astype(BF)

        turn_in(l, wf, gbuf, emit)
        hook(l)

    def zero(e):
        mix[0:896, e] = nn(w0t[...], R[0:896, e])
        scalar = mix[0:128, e].astype(BF)
        gate[:, e] = sigmoid(nn(wgt[...], scalar))

    halves(zero)
    for wt, at, n in ((w1t, 896, 768), (w2t, 2432, 640)):
        def pair(e):
            p, m = R[at : at + n, e], R[at + n : at + 2 * n, e]
            mix[at : at + n, e] = nn(wt[0], p) - nn(wt[1], m)
            mix[at + n : at + 2 * n, e] = nn(wt[1], p) + nn(wt[0], m)

        halves(pair)


def send_messages(wf, mix, gate, oht, bk, agg, hook):
    for l in range(7):
        def load(k, c0, e0):
            v = mix[pl.ds(k * 128 + c0, CH), pl.ds(e0, 128)]
            m = v * sigmoid(v) if k == 0 else v * gate[pl.ds(c0, CH), pl.ds(e0, 128)]
            return m.astype(BF).astype(F32)

        turn_out(l, wf, load, bk)
        agg[:, cols(l)] = nt(oht[...], bk[0 : (2 * l + 1) * 128, :]).astype(BF)
        hook(l)


def backward(cot, wf, oht, wg, gbuf, mix, gate, G, gl, direct):
    gl[...] = jnp.zeros_like(gl)
    for l in range(7):
        gbuf[0 : (2 * l + 1) * 128, :] = tn(cot[:, cols(l)], oht[...]).astype(BF)

        def emit(k, v, c0, e0):
            at = (pl.ds(c0, CH), pl.ds(e0, 128))
            x = mix[pl.ds(k * 128 + c0, CH), pl.ds(e0, 128)]
            if k == 0:
                s = sigmoid(x)
                direct[at] = v * s * (1.0 + x * (1.0 - s))
            else:
                G[pl.ds(k * 128 + c0, CH), pl.ds(e0, 128)] = (v * gate[at]).astype(BF)
                gl[at] += v * x

        turn_in(l, wf, gbuf, emit)
    low = (gl[...] * gate[...] * (1.0 - gate[...])).astype(BF)
    G[0:128, :] = (direct[...] + nn(wg[...], low)).astype(BF)
    return low


def weight_grads(R, G, mix, low, g):
    for at in (0, 256, 512, 768):
        wide = min(256, 896 - at)
        out = nt(R[0:896, :], G[at : at + wide, :]).astype(BF)
        for q in range(wide // 128):
            p = at // 128 + q
            g[p * 896 : (p + 1) * 896, :] = out[:, q * 128 : (q + 1) * 128]
    for base, at, n in ((ONE_AT, 896, 768), (TWO_AT, 2432, 640)):
        for lo in range(0, n, 256):
            wide = min(256, n - lo)
            plus, minus = G[at + lo : at + lo + wide, :], G[at + n + lo : at + n + lo + wide, :]
            rp, rm = R[at : at + n, :], R[at + n : at + 2 * n, :]
            for i, out in enumerate((nt(rp, plus) + nt(rm, minus), nt(rp, minus) - nt(rm, plus))):
                out = out.astype(BF)
                for q in range(wide // 128):
                    r = base + (i * (n // 128) + lo // 128 + q) * n
                    g[r : r + n, :] = out[:, q * 128 : (q + 1) * 128]
    g[GATE_AT:USED, :] = nt(mix[0:128, :].astype(BF), low).astype(BF)
    g[USED:TOTAL, :] = jnp.zeros((TOTAL - USED, 128), BF)


def rotated_grads(radt, w0, w1, w2, G, R):
    def scale(v, e):
        n = v.shape[0]
        return (v.reshape(n // 128, 128, v.shape[1]) * radt[:, e][None]).reshape(v.shape).astype(BF)

    def zero(e):
        R[0:896, e] = scale(nn(w0[...], G[0:896, e]), e)

    halves(zero)
    for w, at, n in ((w1, 896, 768), (w2, 2432, 640)):
        def pair(e):
            p, m = G[at : at + n, e], G[at + n : at + 2 * n, e]
            R[at : at + n, e] = scale(nn(w[0], p) + nn(w[1], m), e)
            R[at + n : at + 2 * n, e] = scale(nn(w[0], m) - nn(w[1], p), e)

        halves(pair)


def source_grads(wf, ohs, R, bk, gn, hook):
    for l in range(7):
        def load(k, c0, e0):
            return R[pl.ds(k * 128 + c0, CH), pl.ds(e0, 128)].astype(F32)

        turn_out(l, wf, load, bk)
        gn[:, cols(l)] = nt(ohs[...], bk[0 : (2 * l + 1) * 128, :]).astype(BF)
        hook(l)


HALF = TOTAL // 2
MESH = pl.DeviceIdType.MESH
CUT = 24 * 128
FIRST, REST = slice(0, CUT), slice(CUT, 6272)
COLORS = (
    (0, 2048, (0, 1, 2)),
    (2048, 2048, (1, 2, 0)),
    (4096, 2048, (2, 0, 1)),
    (6144, 2048, (0, 2, 1)),
    (8192, 2048, (1, 0, 2)),
    (10240, 1024, (2, 1, 0)),
)
EARLY, LATE, ALL = (0, 1, 2), (3, 4, 5), (0, 1, 2, 3, 4, 5)
N = len(COLORS)
SLOT_ROWS = sum(3 * (size // 4 + size // 16 + size // 64) for _, size, _ in COLORS)
N_SEMS = 2 * 14 + 2 * 11 + 5 * N + 2 * 9 * N
N_SEND = 56


class Links:
    def __init__(self, send, recv):
        dp, self.g = lax.axis_index("dp"), lax.axis_index("graph")
        self.dp = dp
        self.pos = (dp // 4, self.g % 4, (self.g // 4) * 2 + (dp // 2) % 2)
        self.core = dp % 2
        self.send, self.recv, self.used = send, recv, 0
        self.free = list(range(N_SEND - 1, -1, -1))

    def at(self, x, y, z, core):
        return ((x * 2 + z % 2) * 2 + core, (z // 2) * 4 + y)

    def along(self, axis, step):
        pos = list(self.pos)
        pos[axis] = (pos[axis] + step) % 4
        return self.at(*pos, self.core)

    def other_core(self):
        return self.at(*self.pos, 1 - self.core)

    def greet(self):
        peers = [self.along(axis, step) for axis in range(3) for step in (1, 2, 3)]
        peers.append(self.other_core())
        barrier = pltpu.get_barrier_semaphore()
        for peer in peers:
            pl.semaphore_signal(barrier, inc=1, device_id=peer, device_id_type=MESH)
        pl.semaphore_wait(barrier, len(peers))

    def copy(self, src, dst, peer):
        slot = self.free.pop()
        out = pltpu.make_async_remote_copy(
            src_ref=src, dst_ref=dst, send_sem=self.send.at[slot], recv_sem=self.recv.at[self.used],
            device_id=peer, device_id_type=MESH,
        )
        self.used += 1
        out.start()
        return Sent(self, out, slot)


class Sent:
    def __init__(self, links, out, slot):
        self.links, self.out, self.slot = links, out, slot

    def wait(self):
        self.out.wait()
        self.links.free.append(self.slot)


def done(copies):
    for c in copies:
        c.wait()


def rows16(i, n=16):
    return pl.ds(pl.multiple_of(i * 16, 16), n)


class Gather:
    def __init__(self, links, x, full):
        self.links, self.full = links, full
        y = links.pos[1]
        across = links.g + 4 - 8 * (links.g // 4)
        own, self.other = rows16(links.g), rows16(across)
        self.column = [rows16(links.g - y + (y + 4 - d) % 4) for d in (1, 3, 2)]
        self.over = [links.copy(x.at[:, FIRST], full.at[own, FIRST], links.along(2, 2))]
        self.side = [links.copy(x.at[:, REST], full.at[own, REST], links.along(1, d)) for d in (1, 3, 2)]
        self.last = [links.copy(x.at[:, REST], full.at[own, REST], links.along(2, 2))]
        self.last += [links.copy(x.at[:, FIRST], full.at[own, FIRST], links.along(1, d)) for d in (1, 3, 2)]
        full[own, :] = x[...]

    def relay_over(self):
        done(self.over)
        part = self.full.at[self.other, FIRST]
        self.last += [self.links.copy(part, part, self.links.along(1, d)) for d in (1, 3, 2)]

    def relay_side(self):
        for c, rows in zip(self.side, self.column):
            c.wait()
            part = self.full.at[rows, REST]
            self.last.append(self.links.copy(part, part, self.links.along(2, 2)))

    def finish(self):
        done(self.last)


class Scatter:
    def __init__(self, links, part, out, near, far, send_far, last_far, pile, last_near):
        self.links, self.part, self.out = links, part, out
        self.near, self.far, self.send_far, self.last_far = near, far, send_far, last_far
        self.pile, self.last_near = pile, last_near
        y = links.pos[1]
        self.y = y
        self.here = links.g - y
        self.there = 4 - self.here
        self.a, self.b = [], []
        column = pl.ds(pl.multiple_of(self.there * 16, 16), 64)
        self.b.append(links.copy(part.at[column, REST], pile, links.along(2, 2)))
        for i, d in enumerate((1, 3, 2)):
            peer = (y + d) % 4
            for ref, base in ((far, self.there), (near, self.here)):
                self.a.append(links.copy(part.at[rows16(base + peer), FIRST], ref.at[i], links.along(1, d)))

    def middle(self):
        links, part, y = self.links, self.part, self.y
        done(self.a)
        total = part[rows16(self.there + y), FIRST].astype(F32)
        for i in range(3):
            total += self.far[i].astype(F32)
        self.send_far[...] = total.astype(BF)
        self.last = [links.copy(self.send_far, self.last_far, links.along(2, 2))]
        done(self.b)
        for i in range(4):
            rows = pl.ds(i * 16, 16)
            mine = part[rows16(self.here + i), REST].astype(F32)
            self.pile[rows, :] = (mine + self.pile[rows, :].astype(F32)).astype(BF)
        for i, d in enumerate((1, 3, 2)):
            self.last.append(links.copy(self.pile.at[rows16((y + d) % 4)], self.last_near.at[i], links.along(1, d)))

    def finish(self):
        done(self.last)
        total = self.part[rows16(self.here + self.y), FIRST].astype(F32) + self.last_far[...].astype(F32)
        for i in range(3):
            total += self.near[i].astype(F32)
        self.out[:, FIRST] = total.astype(BF)
        total = self.pile[rows16(self.y), :].astype(F32)
        for i in range(3):
            total += self.last_near[i].astype(F32)
        self.out[:, REST] = total.astype(BF)


def add_rows(dst, d0, srcs, n):
    step = 256 if n % 256 == 0 else n

    def body(t, _):
        total = None
        for ref, r in srcs:
            v = ref[pl.ds(pl.multiple_of(r + t * step, 16), step), :].astype(F32)
            total = v if total is None else total + v
        dst[pl.ds(pl.multiple_of(d0 + t * step, 16), step), :] = total.astype(BF)
        return 0

    if n == step:
        body(0, 0)
    else:
        lax.fori_loop(0, n // step, body, 0)


class SumAll:
    def __init__(self, links, g, inbox, slots, mid, small, full):
        self.links, self.g, self.slots, self.mid, self.small, self.full = links, g, slots, mid, small, full
        self.inbox, self.swaps = inbox, []
        self.home = links.core * HALF
        away = (1 - links.core) * HALF
        self.waiting, self.src, self.place, self.slot_at, at = {}, {}, {}, {}, 0
        for c, (base, size, axes) in enumerate(COLORS):
            self.src[c], self.place[c] = (g, self.home + base), self.home + base
            for s in range(3):
                self.slot_at[c, s] = at
                at += 3 * (size // 4 ** (s + 1))
            rows = pl.ds(pl.multiple_of(away + base, 16), size)
            self.waiting[c] = [links.copy(g.at[rows], inbox.at[pl.ds(base, size)], links.other_core())]

    def swapped(self, c):
        base, size, _ = COLORS[c]
        done(self.waiting[c])
        at = self.home + base
        add_rows(self.g, at, [(self.g, at), (self.inbox, base)], size)

    def sizes(self, c, s):
        return COLORS[c][1] // 4 ** (s + 1), COLORS[c][2][s]

    def start(self, c, s):
        links = self.links
        (n, axis), (ref, row) = self.sizes(c, s), self.src[c]
        out = []
        for d in (1, 3, 2):
            j = (links.pos[axis] + d) % 4
            out.append(links.copy(
                ref.at[pl.ds(pl.multiple_of(row + j * n, 16), n)],
                self.slots.at[pl.ds(self.slot_at[c, s] + (d - 1) * n, n)],
                links.along(axis, d)))
        self.waiting[c] = out

    def reduce(self, c, s):
        (n, axis), (ref, row) = self.sizes(c, s), self.src[c]
        base = COLORS[c][0]
        own = row + self.links.pos[axis] * n
        self.place[c] = self.place[c] + self.links.pos[axis] * n
        done(self.waiting[c])
        srcs = [(ref, own)] + [(self.slots, self.slot_at[c, s] + d * n) for d in range(3)]
        dst, d0 = ((self.mid, base // 4), (self.small, base // 16), (self.full, self.place[c]))[s]
        add_rows(dst, d0, srcs, n)
        self.src[c] = (dst, d0)
        if s < 2:
            self.start(c, s + 1)
        else:
            self.share(c, 2)

    def share(self, c, s):
        n, axis = self.sizes(c, s)
        rows = self.full.at[pl.ds(pl.multiple_of(self.place[c], 16), n)]
        if s < 2:
            done(self.waiting[c])
        self.waiting[c] = [self.links.copy(rows, rows, self.links.along(axis, d)) for d in (1, 3, 2)]
        if s == 0:
            self.swaps.append(self.links.copy(rows, rows, self.links.other_core()))
        self.place[c] = self.place[c] - self.links.pos[axis] * n

    def back(self, c):
        n, axis = self.sizes(c, 0)
        for copy, d in zip(self.waiting[c], (1, 3, 2)):
            copy.wait()
            block = (self.links.pos[axis] + 4 - d) % 4
            rows = self.full.at[pl.ds(pl.multiple_of(self.place[c] + block * n, 16), n)]
            self.swaps.append(self.links.copy(rows, rows, self.links.other_core()))

    def finish(self):
        done(self.swaps)

    def each(self, colors, step, *args):
        for c in colors:
            step(c, *args)


def layer_kernel(x, cx, src, tgt, cnt, wig, rad, w0, w1, w2, wg, agg, gn, full,
                 nodes, cot, w0t, w1t, w2t, wgt, wf, radt, ohs, oht, gbuf, R, mix, G, gate, gl, direct, bk,
                 pagg, near1, far1, send1, last1, pile1, lastn1, near2, far2, send2, last2, pile2, lastn2,
                 g, inbox, slots, mid, small, send, recv):
    links = Links(send, recv)
    links.greet()
    gather = Gather(links, x, nodes)
    prepare(src, tgt, cnt, wig, rad, wf, radt, ohs, oht)
    gather.relay_over()
    turn(w0, w0t)
    turn(w1.at[0], w1t.at[0])
    gather.relay_side()
    turn(w1.at[1], w1t.at[1])
    for i in range(2):
        turn(w2.at[i], w2t.at[i])
    turn(wg, wgt)
    gather.finish()
    gather = Gather(links, cx, cot)

    def hook(l):
        if l == 3:
            gather.relay_over()
        if l == 5:
            gather.relay_side()

    forward(nodes, wf, radt, ohs, w0t, w1t, w2t, wgt, gbuf, R, mix, gate, hook)
    gather.finish()
    low = backward(cot, wf, oht, wg, gbuf, mix, gate, G, gl, direct)
    weight_grads(R, G, mix, low, g)
    total = SumAll(links, g, inbox, slots, mid, small, full)

    def hook(l):
        colors = {3: EARLY, 5: LATE}.get(l, ())
        total.each(colors, total.swapped)
        total.each(colors, total.start, 0)

    send_messages(wf, mix, gate, oht, bk, pagg, hook)
    first = Scatter(links, pagg, agg, near1, far1, send1, last1, pile1, lastn1)
    rotated_grads(radt, w0, w1, w2, G, R)

    def hook(l):
        if l == 2:
            total.each(EARLY, total.reduce, 0)
        if l == 4:
            total.each(LATE, total.reduce, 0)
            first.middle()
        if l == 5:
            total.each(ALL, total.reduce, 1)

    source_grads(wf, ohs, R, bk, nodes, hook)
    second = Scatter(links, nodes, gn, near2, far2, send2, last2, pile2, lastn2)
    total.each(ALL, total.reduce, 2)
    total.each(ALL, total.share, 1)
    first.finish()
    total.each(ALL, total.share, 0)
    second.middle()
    total.each(ALL, total.back)
    second.finish()
    total.finish()


def unpack_kernel(full, agg, gn, agg_o, gn_o, zero, one, two, last, buf, b0, b1, b2, b3, s_in, s_out):
    pieces = [(full.at[pl.ds(lo, hi - lo)], buf.at[pl.ds(lo, hi - lo)]) for lo, hi in zip(BOUNDS[:-1], BOUNDS[1:])]
    loads = [pltpu.make_async_copy(a, b, s_in.at[i]) for i, (a, b) in enumerate(pieces)]
    for c in loads:
        c.start()
    stores = [pltpu.make_async_copy(agg, agg_o, s_out.at[6]), pltpu.make_async_copy(gn, gn_o, s_out.at[7])]
    for c in stores:
        c.start()
    targets = [(b0, zero), (b1.at[0], one.at[0]), (b1.at[1], one.at[1]), (b2.at[0], two.at[0]), (b2.at[1], two.at[1]), (b3, last)]
    for i, (tile, out) in enumerate(targets):
        loads[i].wait()
        n = tile.shape[0]
        for p in range(n // 128):
            at = BOUNDS[i] + p * n
            tile[:, p * 128 : (p + 1) * 128] = buf[at : at + n, :].astype(F32)
        stores.append(pltpu.make_async_copy(tile, out, s_out.at[i]))
        stores[-1].start()
    for c in stores:
        c.wait()


BOUNDS = (0, ONE_AT, ONE_AT + 4608, TWO_AT, TWO_AT + 3200, GATE_AT, USED)


def scatter_scratch():
    first, rest = CUT, 6272 - CUT
    shapes = ((3, 16, first), (3, 16, first), (16, first), (16, first), (64, rest), (3, 16, rest))
    return [pltpu.VMEM(shape, BF) for shape in shapes]


def per_device(nodes, sources, targets, counts, wigner, radial, cotangent, w0, w1, w2, wg):
    vm = pl.BlockSpec(memory_space=pltpu.VMEM)
    hbm = pl.BlockSpec(memory_space=pl.ANY)
    dma = pltpu.SemaphoreType.DMA
    agg, gn, full = pl.pallas_call(
        layer_kernel,
        out_shape=(
            jax.ShapeDtypeStruct((16, 6272), BF),
            jax.ShapeDtypeStruct((16, 6272), BF),
            jax.ShapeDtypeStruct((TOTAL, 128), BF),
        ),
        in_specs=[vm] * 11,
        out_specs=(vm, vm, vm),
        scratch_shapes=[
            pltpu.VMEM((128, 6272), BF),
            pltpu.VMEM((128, 6272), BF),
            pltpu.VMEM((896, 896), BF),
            pltpu.VMEM((2, 768, 768), BF),
            pltpu.VMEM((2, 640, 640), BF),
            pltpu.VMEM((128, 128), BF),
            pltpu.VMEM((4, 49, 40, 128), F32),
            pltpu.VMEM((128, 512), F32),
            pltpu.VMEM((128, 512), BF),
            pltpu.VMEM((128, 512), BF),
            pltpu.VMEM((13 * 128, 512), BF),
            pltpu.VMEM((3712, 512), BF),
            pltpu.VMEM((3712, 512), F32),
            pltpu.VMEM((3712, 512), BF),
            pltpu.VMEM((128, 512), F32),
            pltpu.VMEM((128, 512), F32),
            pltpu.VMEM((128, 512), F32),
            pltpu.VMEM((13 * 128, 512), BF),
            pltpu.VMEM((128, 6272), BF),
            *scatter_scratch(),
            *scatter_scratch(),
            pltpu.VMEM((TOTAL, 128), BF),
            pltpu.VMEM((HALF, 128), BF),
            pltpu.VMEM((SLOT_ROWS, 128), BF),
            pltpu.VMEM((HALF // 4, 128), BF),
            pltpu.VMEM((HALF // 16, 128), BF),
            dma((N_SEND,)),
            dma((N_SEMS,)),
        ],
        compiler_params=pltpu.CompilerParams(
            vmem_limit_bytes=67043328, collective_id=0, has_side_effects=True
        ),
        name="edge_layer",
    )(nodes[0], cotangent[0], sources, targets, counts, jnp.swapaxes(wigner[0], 0, 1), radial[0], w0, w1, w2, wg)
    return_shapes = [(16, 6272)] * 2 + [(896, 896), (2, 768, 768), (2, 640, 640), (128, 128)]
    agg, gn, zero, one, two, last = pl.pallas_call(
        unpack_kernel,
        out_shape=[jax.ShapeDtypeStruct(shape, BF if i < 2 else F32) for i, shape in enumerate(return_shapes)],
        in_specs=[hbm, vm, vm],
        out_specs=[hbm] * 6,
        scratch_shapes=[
            pltpu.VMEM((USED, 128), BF),
            *[pltpu.VMEM(shape, F32) for shape in return_shapes[2:]],
            dma((6,)),
            dma((8,)),
        ],
        compiler_params=pltpu.CompilerParams(vmem_limit_bytes=67043328),
        name="unpack",
    )(full, agg, gn)
    return agg[None], gn[None], zero, one, two, last


def solution(mesh):
    in_specs = (
        P("dp", "graph", None),
        P("dp", "graph"),
        P("dp", "graph"),
        P("dp", "graph"),
        P("dp", None, None, "graph"),
        P("dp", "graph", None),
        P("dp", "graph", None),
        P(),
        P(),
        P(),
        P(),
    )
    out_specs = (P("dp", "graph", None), P("dp", "graph", None), P(), P(), P(), P())
    return jax.shard_map(
        per_device, mesh=mesh, in_specs=in_specs, out_specs=out_specs, check_vma=False
    )
```
